32 devices in a mesh: fsdp: 32 (over z, y, x, core).
Axes of the slice: x: 2, y: 2, z: 4, core: 2. Of those that a mesh axis runs over, the one named last changes fastest.
Arguments:
- tokens: bfloat16 [65536, 640], P('fsdp'), may hold values from -6 to 6
- out_grad: bfloat16 [65536, 640], P('fsdp'), may hold values from -6 to 6
- seq_lengths: int32 [64, 4], P('fsdp'), may hold values from 0 to 1024, as said below
- w_query: bfloat16 [640, 1024], P(None, 'fsdp'), may hold values from -0.25 to 0.25
- w_key: bfloat16 [640, 256], P(None, 'fsdp'), may hold values from -0.25 to 0.25
- w_value: bfloat16 [640, 256], P(None, 'fsdp'), may hold values from -0.25 to 0.25
- w_output: bfloat16 [640, 1024], P(None, 'fsdp'), may hold values from -0.1875 to 0.1875
- w_gate: bfloat16 [640, 2048], P(None, 'fsdp'), may hold values from -0.25 to 0.25
- w_up: bfloat16 [640, 2048], P(None, 'fsdp'), may hold values from -0.25 to 0.25
- w_down: bfloat16 [640, 2048], P(None, 'fsdp'), may hold values from -0.125 to 0.125
- gain_input: float32 [640], replicated, may hold values from 0.25 to 1.75
- gain_query: float32 [256], replicated, may hold values from 0.25 to 1.75
- gain_key: float32 [256], replicated, may hold values from 0.25 to 1.75
- gain_attn: float32 [640], replicated, may hold values from 0.25 to 1.75
- gain_ffn_in: float32 [640], replicated, may hold values from 0.25 to 1.75
- gain_ffn_out: float32 [640], replicated, may hold values from 0.25 to 1.75
Outputs:
- output: bfloat16 [65536, 640], P('fsdp')
- grad_tokens: bfloat16 [65536, 640], P('fsdp')
- grad_w_query: float32 [640, 1024], P(None, 'fsdp')
- grad_w_key: float32 [640, 256], P(None, 'fsdp')
- grad_w_value: float32 [640, 256], P(None, 'fsdp')
- grad_w_output: float32 [640, 1024], P(None, 'fsdp')
- grad_w_gate: float32 [640, 2048], P(None, 'fsdp')
- grad_w_up: float32 [640, 2048], P(None, 'fsdp')
- grad_w_down: float32 [640, 2048], P(None, 'fsdp')
- grad_gain_input: float32 [640], replicated
- grad_gain_query: float32 [256], replicated
- grad_gain_key: float32 [256], replicated
- grad_gain_attn: float32 [640], replicated
- grad_gain_ffn_in: float32 [640], replicated
- grad_gain_ffn_out: float32 [640], replicated
The draws below stay inside these ranges and needn't reach their ends.
Inputs may be any that keep to these rules, and one draw needn't show every extreme that they name: `seq_lengths`: row s lists the lengths of up to 4 sequences packed in order into slot s; zeros are empty entries and a row sums to at most 1024. In every draw some slot holds one sequence of exactly 1024 tokens.
All inputs are finite; a program needn't handle non-finite values.
Results may differ from the reference program's by a relative error of at most 0.015.
Values may be sent and summed in bfloat16 or wider, within the bound.
No kernel may reach another device: no remote copies, remote signals or barrier semaphores. Data moves between devices by JAX's collectives and lax.ppermute only.
A program may use at most 256 MiB of HBM per device.

```python
import math
import jax
import jax.numpy as jnp
from jax import lax

D = 640
HEADS = 4
HEAD_DIM = 256
FF = 2048
ROWS = 1024
SLOT_SEQS = 4
SLOTS = 64
TOKENS = 65536


def draw_seq_lengths(key, part):
    key_fill, key_cuts, key_pick = jax.random.split(jax.random.fold_in(key, 17), 3)
    totals = jax.random.randint(key_fill, (SLOTS, 1), ROWS // 8, ROWS + 1)
    cut_points = jax.random.randint(key_cuts, (SLOTS, SLOT_SEQS - 1), 0, totals + 1)
    cut_points = jnp.sort(cut_points, axis=1)
    bounds = jnp.concatenate([jnp.zeros((SLOTS, 1), jnp.int32), cut_points, totals], axis=1)
    lengths = bounds[:, 1:] - bounds[:, :-1]
    picked = jax.random.randint(key_pick, (), 0, SLOTS)
    full_slot = jnp.zeros((SLOT_SEQS,), jnp.int32).at[0].set(ROWS)
    slot_grid = lax.broadcasted_iota(jnp.int32, (SLOTS, SLOT_SEQS), 0)
    return jnp.where(slot_grid == picked, full_slot[None, :], lengths).astype(jnp.int32)


def levels(stream_key, extent, pieces, smallest, largest):
    gain, own = 1.0, jax.random.fold_in(stream_key, 6)
    for dim, blocks in pieces:
        heights = jnp.exp(jax.random.uniform(jax.random.fold_in(own, dim), (blocks,), jnp.float32, smallest / len(pieces), largest / len(pieces)))
        gain = gain * jnp.repeat(heights, extent[dim] // blocks).reshape([-1 if axis == dim else 1 for axis in range(len(extent))])
    return gain


def normal_values(stream_key, extent, width, reach, shards=(), kind=jnp.bfloat16):
    loudness = levels(stream_key, extent, shards, -0.22, 0.18) if shards else 1.0
    values = jax.random.normal(stream_key, extent, jnp.float32) * width * loudness
    return jnp.minimum(jnp.maximum(values, -reach), reach).astype(kind)


def setup_inputs(seed: int = 0) -> dict:
    streams_of = jax.random.split(jax.random.key(seed), 17)
    tokens = normal_values(streams_of[0], (TOKENS, D), 1.0, 6.0, ((0, 32),))
    out_grad = normal_values(streams_of[1], (TOKENS, D), 1.0, 6.0, ((0, 32),))
    seq_lengths = draw_seq_lengths(jax.random.fold_in(streams_of[16], 71), 0)
    w_query = normal_values(streams_of[3], (D, HEADS * HEAD_DIM), D ** -0.5, 0.25, ((1, 32),))
    w_key = normal_values(streams_of[4], (D, HEAD_DIM), D ** -0.5, 0.25, ((1, 32),))
    w_value = normal_values(streams_of[5], (D, HEAD_DIM), D ** -0.5, 0.25, ((1, 32),))
    w_output = normal_values(streams_of[6], (D, HEADS * HEAD_DIM), (HEADS * HEAD_DIM) ** -0.5, 0.1875, ((1, 32),))
    w_gate = normal_values(streams_of[7], (D, FF), D ** -0.5, 0.25, ((1, 32),))
    w_up = normal_values(streams_of[8], (D, FF), D ** -0.5, 0.25, ((1, 32),))
    w_down = normal_values(streams_of[9], (D, FF), FF ** -0.5, 0.125, ((1, 32),))
    gain_input = jnp.clip(1.0 + 0.15 * jax.random.normal(streams_of[10], (D,), jnp.float32), 0.25, 1.75)
    gain_query = jnp.clip(1.0 + 0.15 * jax.random.normal(streams_of[11], (HEAD_DIM,), jnp.float32), 0.25, 1.75)
    gain_key = jnp.clip(1.0 + 0.15 * jax.random.normal(streams_of[12], (HEAD_DIM,), jnp.float32), 0.25, 1.75)
    gain_attn = jnp.clip(1.0 + 0.15 * jax.random.normal(streams_of[13], (D,), jnp.float32), 0.25, 1.75)
    gain_ffn_in = jnp.clip(1.0 + 0.15 * jax.random.normal(streams_of[14], (D,), jnp.float32), 0.25, 1.75)
    gain_ffn_out = jnp.clip(1.0 + 0.15 * jax.random.normal(streams_of[15], (D,), jnp.float32), 0.25, 1.75)
    return {"tokens": tokens, "out_grad": out_grad, "seq_lengths": seq_lengths, "w_query": w_query, "w_key": w_key, "w_value": w_value, "w_output": w_output, "w_gate": w_gate, "w_up": w_up, "w_down": w_down, "gain_input": gain_input, "gain_query": gain_query, "gain_key": gain_key, "gain_attn": gain_attn, "gain_ffn_in": gain_ffn_in, "gain_ffn_out": gain_ffn_out}


EPSILON = 1e-06
ROPE_BASE = 1000000.0
NEG_FILL = -1e+30
QUERY_SCALE = 0.0625
PRECISE = lax.Precision.HIGHEST

@jax.custom_vjp
def low(v):
    return lax.optimization_barrier(v.astype(jnp.bfloat16)).astype(jnp.float32)

@jax.custom_vjp
def low_back(v):
    return v

def low_keep(v):
    return (low(v), None)

def low_pass(kept, grad):
    return (grad,)

def back_keep(v):
    return (v, None)

def back_low(kept, grad):
    return (low(grad),)
low.defvjp(low_keep, low_pass)
low_back.defvjp(back_keep, back_low)

def norm_rows(values, scales):
    return values * lax.rsqrt(lax.optimization_barrier(jnp.mean(values * values, axis=-1, keepdims=True)) + EPSILON) * scales

def rotate_half(values):
    middle = values.shape[-1] // 2
    return jnp.concatenate([-values[..., middle:], values[..., :middle]], axis=-1)

def slot_layout(lengths, row_count):
    seq_ends = jnp.cumsum(lengths, dtype=jnp.int32)
    row_grid = lax.broadcasted_iota(jnp.int32, (row_count, lengths.shape[0]), 0)
    passed = row_grid >= seq_ends[None, :]
    segment = lax.optimization_barrier(jnp.sum(passed.astype(jnp.int32), axis=1, dtype=jnp.int32))
    start_row = lax.optimization_barrier(jnp.sum(jnp.where(passed, lengths[None, :], 0), axis=1, dtype=jnp.int32))
    position = lax.iota(jnp.int32, row_count) - start_row
    return (segment.astype(jnp.int32), position.astype(jnp.int32))

def rope_tables(position):
    freq_index = lax.iota(jnp.int32, HEAD_DIM // 2).astype(jnp.float32)
    inverse = jnp.exp(freq_index * (-2.0 * math.log(ROPE_BASE) / HEAD_DIM))
    phases = position.astype(jnp.float32)[:, None] * inverse[None, :]
    phases = jnp.concatenate([phases, phases], axis=1)
    return (jnp.cos(phases), jnp.sin(phases))

def causal_mask(segment):
    row_count = segment.shape[0]
    query_rows = lax.broadcasted_iota(jnp.int32, (row_count, row_count), 0)
    key_rows = lax.broadcasted_iota(jnp.int32, (row_count, row_count), 1)
    return (segment[:, None] == segment[None, :]) & (key_rows <= query_rows)

def layer_forward(inputs, params, segment, position):
    w_query, w_key, w_value, w_output, w_gate, w_up, w_down, gain_input, gain_query, gain_key, gain_attn, gain_ffn_in, gain_ffn_out = params
    row_count = inputs.shape[0]
    cos_table, sin_table = rope_tables(position)
    normed = low(norm_rows(inputs, gain_input))
    query_raw = low_back(jnp.dot(normed, w_query, precision=PRECISE))
    key_raw = low_back(jnp.dot(normed, w_key, precision=PRECISE))
    value_rows = low(low_back(jnp.dot(normed, w_value, precision=PRECISE)))
    query_norm = norm_rows(query_raw.reshape(row_count, HEADS, HEAD_DIM), gain_query)
    query_rot = low((query_norm * cos_table[:, None] + rotate_half(query_norm) * sin_table[:, None]) * QUERY_SCALE)
    key_norm = norm_rows(key_raw, gain_key)
    key_rot = low(key_norm * cos_table + rotate_half(key_norm) * sin_table)
    scores = low_back(jnp.einsum('qhd,kd->hqk', query_rot, key_rot, precision=PRECISE))
    allowed = causal_mask(segment)
    attn_probs = jax.nn.softmax(jnp.where(allowed[None], scores, NEG_FILL), axis=-1)
    attended = jnp.einsum('hqk,kd->qhd', low(attn_probs), value_rows, precision=PRECISE)
    attended = low(low_back(attended)).reshape(row_count, HEADS * HEAD_DIM)
    branch = low_back(jnp.dot(attended, w_output.T, precision=PRECISE))
    middle = inputs + norm_rows(branch, gain_attn)
    ffn_in = low(norm_rows(middle, gain_ffn_in))
    gate_pre = low_back(jnp.dot(ffn_in, w_gate, precision=PRECISE))
    up_pre = low_back(jnp.dot(ffn_in, w_up, precision=PRECISE))
    hidden = low(jax.nn.gelu(gate_pre, approximate=True) * up_pre)
    ffn_out = low_back(jnp.dot(hidden, w_down.T, precision=PRECISE))
    return middle + norm_rows(ffn_out, gain_ffn_out)

def reference(tokens, out_grad, seq_lengths, w_query, w_key, w_value, w_output, w_gate, w_up, w_down, gain_input, gain_query, gain_key, gain_attn, gain_ffn_in, gain_ffn_out):
    params = tuple((weight.astype(jnp.float32) for weight in (w_query, w_key, w_value, w_output, w_gate, w_up, w_down, gain_input, gain_query, gain_key, gain_attn, gain_ffn_in, gain_ffn_out)))
    token_slots = tokens.astype(jnp.float32).reshape(SLOTS, ROWS, D)
    grad_slots = out_grad.astype(jnp.float32).reshape(SLOTS, ROWS, D)

    def slot_step(running, slot_data):
        inputs, upstream, lengths = slot_data
        segment, position = slot_layout(lengths, ROWS)
        live = (segment < SLOT_SEQS).astype(jnp.float32)
        result, pullback = jax.vjp(lambda inputs_in, params_in: layer_forward(inputs_in, params_in, segment, position), inputs, params)
        grad_inputs, grad_params = pullback(upstream * live[:, None])
        running = tuple((previous + addend for previous, addend in zip(running, grad_params)))
        return (running, (result.astype(jnp.bfloat16), grad_inputs.astype(jnp.bfloat16)))
    zeros_init = tuple((jnp.zeros(weight.shape, jnp.float32) for weight in params))
    totals, (result_slots, grad_input_slots) = lax.scan(slot_step, zeros_init, (token_slots, grad_slots, seq_lengths))
    return (result_slots.reshape(TOKENS, D), grad_input_slots.reshape(TOKENS, D), totals[0], totals[1], totals[2], totals[3], totals[4], totals[5], totals[6], totals[7], totals[8], totals[9], totals[10], totals[11], totals[12])
```

```python
import functools
import math

import jax
import jax.numpy as jnp
from jax import lax
from jax.experimental import pallas as pl
from jax.experimental.pallas import tpu as pltpu
from jax.sharding import PartitionSpec as P

HEADS = 4
HEAD_DIM = 256
HALF = HEAD_DIM // 2
EPSILON = 1e-06
ROPE_BASE = 1000000.0
NEG_FILL = -1e30
QUERY_SCALE = 0.0625
GELU_C = math.sqrt(2.0 / math.pi)
GELU_A = 0.044715
BF = jnp.bfloat16
F32 = jnp.float32
QBLOCK = 256
ROW_BLOCK = 512
FF_CHUNK = 512
VMEM_LIMIT = 60 * 1024 * 1024


def dot_nn(a, b):
    return lax.dot_general(a, b, (((1,), (0,)), ((), ())), preferred_element_type=F32)


def dot_nt(a, b):
    return lax.dot_general(a, b, (((1,), (1,)), ((), ())), preferred_element_type=F32)


def dot_tn(a, b):
    return lax.dot_general(a, b, (((0,), (0,)), ((), ())), preferred_element_type=F32)


def inv_rms(v):
    return lax.rsqrt(jnp.mean(v * v, axis=-1, keepdims=True) + EPSILON)


def row_sum(v):
    return jnp.sum(v, axis=0, keepdims=True)


def params(limit=VMEM_LIMIT):
    return pltpu.CompilerParams(dimension_semantics=("arbitrary",), vmem_limit_bytes=limit)


def const_spec(shape):
    zeros = (0,) * len(shape)
    return pl.BlockSpec(shape, lambda i, *_: zeros, pipeline_mode=pl.Buffered(1))


def cost(flops, nbytes, trans=0):
    return pl.CostEstimate(flops=int(flops), bytes_accessed=int(nbytes), transcendentals=int(trans))


def qkv_kernel(x_ref, w_ref, gi_ref, gq_ref, gk_ref, cos_ref, sin_ref, q_ref, k_ref, v_ref, s_ref, n_ref):
    x = x_ref[...].astype(F32)
    normed = (x * inv_rms(x) * gi_ref[...]).astype(BF)
    n_ref[...] = normed
    cos = cos_ref[...]
    sin = sin_ref[...]
    width = HEADS * HEAD_DIM
    v_ref[...] = dot_nt(normed, w_ref[width + HEAD_DIM :, :]).astype(BF)
    lane = lax.broadcasted_iota(jnp.int32, s_ref.shape, 1)
    saved = jnp.zeros(s_ref.shape, F32)
    for h in range(HEADS + 1):
        raw = dot_nt(normed, w_ref[h * HEAD_DIM : (h + 1) * HEAD_DIM, :])
        inv = inv_rms(raw)
        saved = jnp.where(lane == h, inv, saved)
        gain = gq_ref[...] * QUERY_SCALE if h < HEADS else gk_ref[...]
        y = raw * inv * gain
        y1 = y[:, :HALF]
        y2 = y[:, HALF:]
        out = q_ref.at[h] if h < HEADS else k_ref
        out[:, :HALF] = (y1 * cos - y2 * sin).astype(BF)
        out[:, HALF:] = (y2 * cos + y1 * sin).astype(BF)
    s_ref[...] = saved


def qkv_call(x, w_qkv, gi, gq, gk, cos, sin):
    rows, d = x.shape
    b = ROW_BLOCK
    width = HEADS * HEAD_DIM
    row = lambda n: pl.BlockSpec((b, n), lambda i: (i, 0))
    return pl.pallas_call(
        qkv_kernel,
        grid=(rows // b,),
        in_specs=[row(d), const_spec(w_qkv.shape), const_spec((1, d)), const_spec((1, HEAD_DIM)),
                  const_spec((1, HEAD_DIM)), row(HALF), row(HALF)],
        out_specs=[pl.BlockSpec((HEADS, b, HEAD_DIM), lambda i: (0, i, 0)), row(HEAD_DIM), row(HEAD_DIM),
                   row(128), row(d)],
        out_shape=[jax.ShapeDtypeStruct((HEADS, rows, HEAD_DIM), BF), jax.ShapeDtypeStruct((rows, HEAD_DIM), BF),
                   jax.ShapeDtypeStruct((rows, HEAD_DIM), BF), jax.ShapeDtypeStruct((rows, 128), F32),
                   jax.ShapeDtypeStruct((rows, d), BF)],
        compiler_params=params(),
        cost_estimate=cost(2 * rows * d * (width + 2 * HEAD_DIM), 12 * rows * d),
        name="qkv_rows",
    )(x, w_qkv, gi, gq, gk, cos, sin)


def attend_kernel(blocks, first_ref, q_ref, k_ref, v_ref, start_ref, p_ref, o_ref):
    i = pl.program_id(0)
    qb = lax.rem(i, blocks)
    first = first_ref[i]
    count = qb + 1 - first
    m_rows = HEADS * QBLOCK
    for n in range(1, blocks + 1):

        @pl.when(count == n)
        def _():
            base = pl.multiple_of(first * QBLOCK, QBLOCK)
            window = pl.ds(base, n * QBLOCK)
            q = q_ref[...].reshape(m_rows, HEAD_DIM)
            scores = dot_nt(q, k_ref[window, :])
            col = lax.broadcasted_iota(jnp.int32, scores.shape, 1) + base
            row = lax.broadcasted_iota(jnp.int32, (QBLOCK, 1), 0) + qb * QBLOCK
            row = jnp.concatenate([row] * HEADS, axis=0)
            start = jnp.concatenate([start_ref[...]] * HEADS, axis=0)
            scores = jnp.where((col >= start) & (col <= row), scores, NEG_FILL)
            e = jnp.exp(scores - jnp.max(scores, axis=-1, keepdims=True))
            probs = (e * (1.0 / jnp.sum(e, axis=-1, keepdims=True))).astype(BF)
            p_ref[0, :, : n * QBLOCK] = probs
            out = dot_nn(probs, v_ref[window, :]).astype(BF)
            for h in range(HEADS):
                o_ref[:, h * HEAD_DIM : (h + 1) * HEAD_DIM] = out[h * QBLOCK : (h + 1) * QBLOCK]


def attend_call(first, q, k, v, start, slots):
    rows = k.shape[0]
    slot_rows = rows // slots
    blocks = slot_rows // QBLOCK
    width = HEADS * HEAD_DIM
    slot = pl.BlockSpec((slot_rows, HEAD_DIM), lambda i, *_: (i // blocks, 0))
    return pl.pallas_call(
        functools.partial(attend_kernel, blocks),
        grid_spec=pltpu.PrefetchScalarGridSpec(
            num_scalar_prefetch=1,
            grid=(slots * blocks,),
            in_specs=[pl.BlockSpec((HEADS, QBLOCK, HEAD_DIM), lambda i, *_: (0, i, 0)), slot, slot,
                      pl.BlockSpec((QBLOCK, 1), lambda i, *_: (i, 0))],
            out_specs=[pl.BlockSpec((1, HEADS * QBLOCK, slot_rows), lambda i, *_: (i, 0, 0)),
                       pl.BlockSpec((QBLOCK, width), lambda i, *_: (i, 0))],
        ),
        out_shape=[jax.ShapeDtypeStruct((slots * blocks, HEADS * QBLOCK, slot_rows), BF),
                   jax.ShapeDtypeStruct((rows, width), BF)],
        compiler_params=params(),
        cost_estimate=cost(4 * rows * slot_rows * width * 5 // 8, 2 * rows * slot_rows * HEADS + 8 * rows * width,
                           rows * slot_rows * HEADS * 5 // 8),
        name="attend_rows",
    )(first, q, k, v, start)


def ffn_kernel(slot_rows, total_ref, a_ref, x_ref, og_ref, wo_ref, wg_ref, wu_ref, wd_ref, ga_ref, gf_ref, go_ref,
               out_ref, hid_ref, gg_ref, gu_ref, fin_ref, gfo_ref, gb_ref, gatt_ref, gm_ref, dg_ref,
               gate_s, up_s, acc_s):
    i = pl.program_id(0)
    b = x_ref.shape[0]
    chunks = wg_ref.shape[0] // FF_CHUNK

    @pl.when(i == 0)
    def _():
        dg_ref[...] = jnp.zeros_like(dg_ref)

    branch = dot_nn(a_ref[...], wo_ref[...])
    s_b = inv_rms(branch)
    nb = branch * s_b
    middle = x_ref[...].astype(F32) + nb * ga_ref[...]
    s_m = inv_rms(middle)
    nm = middle * s_m
    ffn_in = (nm * gf_ref[...]).astype(BF)
    fin_ref[...] = ffn_in

    acc_s[...] = jnp.zeros_like(acc_s)

    def forward(c, carry):
        rows = pl.ds(pl.multiple_of(c * FF_CHUNK, FF_CHUNK), FF_CHUNK)
        gate = dot_nt(fin_ref[...], wg_ref[rows, :])
        up = dot_nt(fin_ref[...], wu_ref[rows, :])
        gate_s[c] = gate
        up_s[c] = up
        t = jnp.tanh(gate * (GELU_C + (GELU_C * GELU_A) * (gate * gate)))
        hidden = (0.5 * gate * (1.0 + t) * up).astype(BF)
        hid_ref[c] = hidden
        acc_s[...] += dot_nn(hidden, wd_ref[rows, :])
        return carry

    lax.fori_loop(0, chunks, forward, 0)
    ffn_out = acc_s[...]
    s_f = inv_rms(ffn_out)
    nf = ffn_out * s_f
    out_ref[...] = (middle + nf * go_ref[...]).astype(BF)

    per_slot = slot_rows // b
    row = lax.broadcasted_iota(jnp.int32, (b, 1), 0) + lax.rem(i, per_slot) * b
    live = row < total_ref[i // per_slot]
    upstream = jnp.where(live, og_ref[...].astype(F32), 0.0)
    dg_fo = row_sum(upstream * nf)
    scaled = upstream * go_ref[...]
    gfo = (s_f * (scaled - nf * jnp.mean(scaled * nf, axis=-1, keepdims=True))).astype(BF)
    gfo_ref[...] = gfo
    acc_s[...] = jnp.zeros_like(acc_s)

    def backward(c, carry):
        rows = pl.ds(pl.multiple_of(c * FF_CHUNK, FF_CHUNK), FF_CHUNK)
        gh = dot_nt(gfo_ref[...], wd_ref[rows, :])
        gate = gate_s[c]
        sq = gate * gate
        t = jnp.tanh(gate * (GELU_C + (GELU_C * GELU_A) * sq))
        half_t = 0.5 + 0.5 * t
        slope = half_t + (0.5 * gate) * (1.0 - t * t) * (GELU_C + (3.0 * GELU_C * GELU_A) * sq)
        gg = (gh * up_s[c] * slope).astype(BF)
        gu = (gh * (gate * half_t)).astype(BF)
        gg_ref[c] = gg
        gu_ref[c] = gu
        acc_s[...] += dot_nn(gg, wg_ref[rows, :]) + dot_nn(gu, wu_ref[rows, :])
        return carry

    lax.fori_loop(0, chunks, backward, 0)
    gfin = acc_s[...]
    dg_fi = row_sum(gfin * nm)
    scaled = gfin * gf_ref[...]
    gm = upstream + s_m * (scaled - nm * jnp.mean(scaled * nm, axis=-1, keepdims=True))
    gm_ref[...] = gm
    dg_at = row_sum(gm * nb)
    scaled = gm * ga_ref[...]
    gb = (s_b * (scaled - nb * jnp.mean(scaled * nb, axis=-1, keepdims=True))).astype(BF)
    gb_ref[...] = gb
    gatt_ref[...] = dot_nt(gb, wo_ref[...]).astype(BF)
    dg_ref[0:1, :] += dg_fo
    dg_ref[1:2, :] += dg_fi
    dg_ref[2:3, :] += dg_at


def ffn_call(total, attended, x, og, wo, wg, wu, wd, ga, gf, go, slots):
    rows, d = x.shape
    ff = wg.shape[0]
    width = wo.shape[0]
    b = ROW_BLOCK
    chunks = ff // FF_CHUNK
    row = lambda n: pl.BlockSpec((b, n), lambda i, *_: (i, 0))
    wide = pl.BlockSpec((chunks, b, FF_CHUNK), lambda i, *_: (0, i, 0))
    vec = const_spec((1, d))
    sds = jax.ShapeDtypeStruct
    return pl.pallas_call(
        functools.partial(ffn_kernel, rows // slots),
        grid_spec=pltpu.PrefetchScalarGridSpec(
            num_scalar_prefetch=1,
            grid=(rows // b,),
            in_specs=[row(width), row(d), row(d), const_spec(wo.shape), const_spec(wg.shape), const_spec(wu.shape),
                      const_spec(wd.shape), vec, vec, vec],
            out_specs=[row(d), wide, wide, wide, row(d), row(d), row(d), row(width), row(d),
                       pl.BlockSpec((8, d), lambda i, *_: (0, 0))],
            scratch_shapes=[pltpu.VMEM((chunks, b, FF_CHUNK), F32), pltpu.VMEM((chunks, b, FF_CHUNK), F32),
                            pltpu.VMEM((b, d), F32)],
        ),
        out_shape=[sds((rows, d), BF), sds((chunks, rows, FF_CHUNK), BF), sds((chunks, rows, FF_CHUNK), BF),
                   sds((chunks, rows, FF_CHUNK), BF), sds((rows, d), BF), sds((rows, d), BF), sds((rows, d), BF),
                   sds((rows, width), BF), sds((rows, d), F32), sds((8, d), F32)],
        compiler_params=params(),
        cost_estimate=cost(4 * rows * d * (width + 3 * ff), rows * (6 * ff + 12 * d), 2 * rows * ff),
        name="ffn_rows",
    )(total, attended, x, og, wo, wg, wu, wd, ga, gf, go)


def rope_back_halves(g1, g2, cos, sin):
    return g1 * cos + g2 * sin, g2 * cos - g1 * sin


def norm_rope_back(grad, rotated, inv, gain, cos, sin, scale):
    m = jnp.mean(grad * rotated, axis=-1, keepdims=True)
    dy1, dy2 = rope_back_halves(grad[:, :HALF], grad[:, HALF:], cos, sin)
    u1, u2 = rope_back_halves(rotated[:, :HALF], rotated[:, HALF:], cos, sin)
    dy = jnp.concatenate([dy1, dy2], axis=1) * scale
    n = jnp.concatenate([u1, u2], axis=1) * ((1.0 / scale) / gain)
    return inv * (dy * gain - n * m), row_sum(dy * n)


def attend_back_kernel(blocks, first_ref, p_ref, q_ref, k_ref, v_ref, do_ref, s_ref, cos_ref, sin_ref, gq_ref, gk_ref,
                       gqr_ref, gkr_ref, gv_ref, dg_ref, dq_s, dk_s, dv_s):
    i = pl.program_id(0)
    qb = lax.rem(i, blocks)
    first = first_ref[i]
    count = qb + 1 - first
    m_rows = HEADS * QBLOCK

    @pl.when(i == 0)
    def _():
        dg_ref[...] = jnp.zeros_like(dg_ref)

    @pl.when(qb == 0)
    def _():
        dk_s[...] = jnp.zeros_like(dk_s)
        dv_s[...] = jnp.zeros_like(dv_s)

    for n in range(1, blocks + 1):

        @pl.when(count == n)
        def _():
            base = pl.multiple_of(first * QBLOCK, QBLOCK)
            window = pl.ds(base, n * QBLOCK)
            do = jnp.concatenate([do_ref[:, h * HEAD_DIM : (h + 1) * HEAD_DIM] for h in range(HEADS)], axis=0)
            q = q_ref[...].reshape(m_rows, HEAD_DIM)
            probs = p_ref[0, :, : n * QBLOCK]
            dp = dot_nt(do, v_ref[window, :])
            pf = probs.astype(F32)
            total = jnp.sum(pf * dp, axis=-1, keepdims=True)
            ds = (pf * (dp - total)).astype(BF)
            dq_s[...] = dot_nn(ds, k_ref[window, :])
            dk_s[window, :] += dot_tn(ds, q)
            dv_s[window, :] += dot_tn(probs, do)

    rows = pl.ds(pl.multiple_of(qb * QBLOCK, QBLOCK), QBLOCK)
    cos = cos_ref[rows, :]
    sin = sin_ref[rows, :]
    inv = s_ref[rows, :]
    for h in range(HEADS):
        grad, dg = norm_rope_back(dq_s[h * QBLOCK : (h + 1) * QBLOCK, :], q_ref[h].astype(F32), inv[:, h : h + 1],
                                  gq_ref[...], cos, sin, QUERY_SCALE)
        gqr_ref[:, h * HEAD_DIM : (h + 1) * HEAD_DIM] = grad.astype(BF)
        dg_ref[0:1, :] += dg

    @pl.when(qb == blocks - 1)
    def _():
        gv_ref[...] = dv_s[...].astype(BF)
        grad, dg = norm_rope_back(dk_s[...], k_ref[...].astype(F32), s_ref[:, HEADS : HEADS + 1], gk_ref[...],
                                  cos_ref[...], sin_ref[...], 1.0)
        gkr_ref[...] = grad.astype(BF)
        dg_ref[1:2, :] += dg


def attend_back_call(first, p, q, k, v, do, s, cos, sin, gq, gk, slots):
    rows = k.shape[0]
    slot_rows = rows // slots
    blocks = slot_rows // QBLOCK
    width = HEADS * HEAD_DIM
    slot = lambda n: pl.BlockSpec((slot_rows, n), lambda i, *_: (i // blocks, 0))
    block = lambda n: pl.BlockSpec((QBLOCK, n), lambda i, *_: (i, 0))
    sds = jax.ShapeDtypeStruct
    return pl.pallas_call(
        functools.partial(attend_back_kernel, blocks),
        grid_spec=pltpu.PrefetchScalarGridSpec(
            num_scalar_prefetch=1,
            grid=(slots * blocks,),
            in_specs=[pl.BlockSpec((1, HEADS * QBLOCK, slot_rows), lambda i, *_: (i, 0, 0)),
                      pl.BlockSpec((HEADS, QBLOCK, HEAD_DIM), lambda i, *_: (0, i, 0)),
                      slot(HEAD_DIM), slot(HEAD_DIM), block(width), slot(128), slot(HALF), slot(HALF),
                      const_spec((1, HEAD_DIM)), const_spec((1, HEAD_DIM))],
            out_specs=[block(width), slot(HEAD_DIM), slot(HEAD_DIM), pl.BlockSpec((8, HEAD_DIM), lambda i, *_: (0, 0))],
            scratch_shapes=[pltpu.VMEM((HEADS * QBLOCK, HEAD_DIM), F32), pltpu.VMEM((slot_rows, HEAD_DIM), F32),
                            pltpu.VMEM((slot_rows, HEAD_DIM), F32)],
        ),
        out_shape=[sds((rows, width), BF), sds((rows, HEAD_DIM), BF), sds((rows, HEAD_DIM), BF),
                   sds((8, HEAD_DIM), F32)],
        compiler_params=params(),
        cost_estimate=cost(8 * rows * slot_rows * width * 5 // 8, 2 * rows * slot_rows * HEADS + 12 * rows * width),
        name="attend_back_rows",
    )(first, p, q, k, v, do, s, cos, sin, gq, gk)


def input_back_kernel(gq_ref, gk_ref, gv_ref, x_ref, gm_ref, w_ref, gi_ref, gx_ref, dg_ref):
    @pl.when(pl.program_id(0) == 0)
    def _():
        dg_ref[...] = jnp.zeros_like(dg_ref)

    width = HEADS * HEAD_DIM
    gn = dot_nn(gq_ref[...], w_ref[:width, :])
    gn += dot_nn(gk_ref[...], w_ref[width : width + HEAD_DIM, :])
    gn += dot_nn(gv_ref[...], w_ref[width + HEAD_DIM :, :])
    x = x_ref[...].astype(F32)
    inv = inv_rms(x)
    n = x * inv
    dg_ref[0:1, :] += row_sum(gn * n)
    scaled = gn * gi_ref[...]
    gx = inv * (scaled - n * jnp.mean(scaled * n, axis=-1, keepdims=True))
    gx_ref[...] = (gm_ref[...] + gx).astype(BF)


def input_back_call(gq, gk, gv, x, gm, w_qkv, gi):
    rows, d = x.shape
    b = ROW_BLOCK
    row = lambda n: pl.BlockSpec((b, n), lambda i: (i, 0))
    return pl.pallas_call(
        input_back_kernel,
        grid=(rows // b,),
        in_specs=[row(gq.shape[1]), row(HEAD_DIM), row(HEAD_DIM), row(d), row(d), const_spec(w_qkv.shape),
                  const_spec((1, d))],
        out_specs=[row(d), pl.BlockSpec((8, d), lambda i: (0, 0))],
        out_shape=[jax.ShapeDtypeStruct((rows, d), BF), jax.ShapeDtypeStruct((8, d), F32)],
        compiler_params=params(),
        cost_estimate=cost(2 * rows * d * w_qkv.shape[0], 14 * rows * d),
        name="input_back_rows",
    )(gq, gk, gv, x, gm, w_qkv, gi)


def level_list(count):
    levels = [(1, 2)]
    stride = 2
    while stride < count:
        size = 4 if count // stride >= 4 else 2
        levels.append((stride, size))
        stride *= size
    return levels[::-1]


def send(x, count, offset):
    return lax.ppermute(x, "fsdp", [(i, i ^ offset) for i in range(count)])


def gather_blocks(x, count):
    x = x[None]
    for stride, size in level_list(count):
        x = jnp.concatenate([x] + [send(x, count, k * stride) for k in range(1, size)], axis=0)
    return x


def block_offsets(count):
    offsets = [0]
    for stride, size in level_list(count):
        offsets = [o ^ (k * stride) for k in range(size) for o in offsets]
    return offsets


def scatter_blocks(g, count):
    for stride, size in level_list(count)[::-1]:
        g = g.reshape((size, g.shape[0] // size) + g.shape[1:])
        g16 = g.astype(BF)
        total = g[0].astype(F32)
        for k in range(1, size):
            total = total + send(g16[k], count, k * stride).astype(F32)
        g = total
    return g[0]


def sum_small(x, count):
    for stride, size in level_list(count)[::-1]:
        parts = [x] + [send(x, count, k * stride) for k in range(1, size)]
        x = functools.reduce(jnp.add, parts)
    return x


def slot_layout(lengths, row_count):
    seq_ends = jnp.cumsum(lengths, axis=1, dtype=jnp.int32)
    rows = lax.broadcasted_iota(jnp.int32, (lengths.shape[0], row_count), 1)
    passed = rows[:, :, None] >= seq_ends[:, None, :]
    start = jnp.sum(jnp.where(passed, lengths[:, None, :], 0), axis=2, dtype=jnp.int32)
    return start, rows - start, seq_ends[:, -1]


def shards(count, tokens, out_grad, seq_lengths, w_query, w_key, w_value, w_output, w_gate, w_up, w_down,
           gain_input, gain_query, gain_key, gain_attn, gain_ffn_in, gain_ffn_out):
    slots = seq_lengths.shape[0]
    rows, d = tokens.shape
    slot_rows = rows // slots
    me = lax.axis_index("fsdp")
    offsets = jnp.array(block_offsets(count), jnp.int32)
    inverse = [0] * count
    for j, o in enumerate(block_offsets(count)):
        inverse[o] = j
    inverse = jnp.array(inverse, jnp.int32)
    place = inverse[jnp.arange(count, dtype=jnp.int32) ^ me]
    owner = offsets ^ me

    nq, nk, nf = w_query.shape[1], w_key.shape[1], w_gate.shape[1]
    own_qkv = jnp.concatenate([w_query.T, w_key.T, w_value.T], axis=0)
    all_qkv = gather_blocks(own_qkv, count)
    all_out = gather_blocks(w_output.T, count)
    own_ffn = jnp.concatenate([w_gate.T, w_up.T, w_down.T], axis=0)
    all_ffn = gather_blocks(own_ffn, count)

    start, position, total = slot_layout(seq_lengths, slot_rows)
    inv_freq = jnp.exp(lax.iota(jnp.int32, HALF).astype(F32) * (-2.0 * math.log(ROPE_BASE) / HEAD_DIM))
    phases = position.reshape(rows, 1).astype(F32) * inv_freq[None, :]
    cos = jnp.cos(phases)
    sin = jnp.sin(phases)
    first = (start[:, ::QBLOCK] // QBLOCK).reshape(-1)
    start_col = start.reshape(rows, 1)
    gi, gq, gk = gain_input[None], gain_query[None], gain_key[None]

    all_qkv = all_qkv[place]
    w_qkv = jnp.concatenate(
        [all_qkv[:, :nq].reshape(-1, d), all_qkv[:, nq : nq + nk].reshape(-1, d), all_qkv[:, nq + nk :].reshape(-1, d)],
        axis=0,
    )
    q, k, v, s, normed = qkv_call(tokens, w_qkv, gi, gq, gk, cos, sin)
    p, attended = attend_call(first, q, k, v, start_col, slots)

    wo = all_out[place].reshape(-1, d)
    wg = all_ffn[:, :nf].reshape(-1, d)
    wu = all_ffn[:, nf : 2 * nf].reshape(-1, d)
    wd = all_ffn[:, 2 * nf :].reshape(-1, d)
    out, hid, gg, gu, fin, gfo, gb, gatt, gm, dg_ffn = ffn_call(
        total, attended, tokens, out_grad, wo, wg, wu, wd, gain_attn[None], gain_ffn_in[None], gain_ffn_out[None], slots
    )

    def wide_grad(a, b):
        return lax.dot_general(a, b, (((1,), (0,)), ((), ())), preferred_element_type=F32).astype(BF).reshape(count, nf, d)

    g_down = scatter_blocks(wide_grad(hid, gfo), count)
    g_gate = scatter_blocks(wide_grad(gg, fin), count)
    g_up = scatter_blocks(wide_grad(gu, fin), count)
    g_out = dot_tn(attended, gb).astype(BF).reshape(count, nq, d)
    g_out = scatter_blocks(g_out[owner], count)

    gqr, gkr, gv, dg_att = attend_back_call(first, p, q, k, v, gatt, s, cos, sin, gq, gk, slots)
    g_q = dot_tn(gqr, normed).astype(BF).reshape(count, nq, d)
    g_k = dot_tn(gkr, normed).astype(BF).reshape(count, nk, d)
    g_v = dot_tn(gv, normed).astype(BF).reshape(count, nk, d)
    g_qkv = jnp.concatenate([g_q, g_k, g_v], axis=1)[owner]
    g_qkv = scatter_blocks(g_qkv, count)

    grad_tokens, dg_in = input_back_call(gqr, gkr, gv, tokens, gm, w_qkv, gi)
    gains = jnp.concatenate([dg_in[0], dg_att[0], dg_att[1], dg_ffn[2], dg_ffn[1], dg_ffn[0]])
    gains = sum_small(gains.reshape(-1, 128), count).reshape(-1)
    h = HEAD_DIM
    return (
        out,
        grad_tokens,
        g_qkv[:nq].T,
        g_qkv[nq : nq + nk].T,
        g_qkv[nq + nk :].T,
        g_out.T,
        g_gate.T,
        g_up.T,
        g_down.T,
        gains[:d],
        gains[d : d + h],
        gains[d + h : d + 2 * h],
        gains[d + 2 * h : 2 * d + 2 * h],
        gains[2 * d + 2 * h : 3 * d + 2 * h],
        gains[3 * d + 2 * h :],
    )


def solution(mesh):
    split_rows = P("fsdp", None)
    split_cols = P(None, "fsdp")
    return jax.shard_map(
        functools.partial(shards, mesh.shape["fsdp"]),
        mesh=mesh,
        in_specs=(split_rows,) * 3 + (split_cols,) * 7 + (P(),) * 6,
        out_specs=(split_rows,) * 2 + (split_cols,) * 7 + (P(),) * 6,
        check_vma=False,
    )
```

```python
import functools
import math

import jax
import jax.numpy as jnp
from jax import lax
from jax.experimental import pallas as pl
from jax.experimental.pallas import tpu as pltpu
from jax.sharding import PartitionSpec as P

HEADS = 4
HEAD_DIM = 256
HALF = HEAD_DIM // 2
EPSILON = 1e-06
ROPE_BASE = 1000000.0
NEG_FILL = -1e30
QUERY_SCALE = 0.0625
GELU_C = math.sqrt(2.0 / math.pi)
GELU_A = 0.044715
BF = jnp.bfloat16
F32 = jnp.float32
QBLOCK = 256
ROW_BLOCK = 512
FF_BLOCK = 512
FFN_ROWS = 256
VMEM_LIMIT = 60 * 1024 * 1024


def dot_nn(a, b):
    return lax.dot_general(a, b, (((1,), (0,)), ((), ())), preferred_element_type=F32)


def dot_nt(a, b):
    return lax.dot_general(a, b, (((1,), (1,)), ((), ())), preferred_element_type=F32)


def dot_tn(a, b):
    return lax.dot_general(a, b, (((0,), (0,)), ((), ())), preferred_element_type=F32)


def inv_rms(v):
    return lax.rsqrt(jnp.mean(v * v, axis=-1, keepdims=True) + EPSILON)


def row_sum(v):
    return jnp.sum(v, axis=0, keepdims=True)


def params(limit=VMEM_LIMIT):
    return pltpu.CompilerParams(dimension_semantics=("arbitrary",), vmem_limit_bytes=limit)


def const_spec(shape):
    zeros = (0,) * len(shape)
    return pl.BlockSpec(shape, lambda i, *_: zeros, pipeline_mode=pl.Buffered(1))


def cost(flops, nbytes, trans=0):
    return pl.CostEstimate(flops=int(flops) // 32, bytes_accessed=int(nbytes) // 32, transcendentals=int(trans) // 32)


def pack_qkv(place_ref, own_ref, other_ref, w_ref, nq, nk):
    half = own_ref.shape[0]
    width = HEADS * HEAD_DIM
    per = 16 // nk

    def group(g, carry):
        keys = []
        values = []
        for e in range(per):
            j = g * per + e
            at = place_ref[j]
            low = jnp.minimum(at, half - 1)
            high = jnp.maximum(at - half, 0)
            block = jnp.where(at < half, own_ref[low].astype(F32), other_ref[high].astype(F32))
            w_ref[pl.ds(pl.multiple_of(j * nq, nq), nq), :] = block[:nq].astype(BF)
            keys.append(block[nq : nq + nk])
            values.append(block[nq + nk :])
        at = pl.multiple_of(width + g * 16, 16)
        w_ref[pl.ds(at, 16), :] = jnp.concatenate(keys, axis=0).astype(BF)
        at = pl.multiple_of(width + HEAD_DIM + g * 16, 16)
        w_ref[pl.ds(at, 16), :] = jnp.concatenate(values, axis=0).astype(BF)
        return carry

    lax.fori_loop(0, 2 * half // per, group, 0)


def qkv_kernel(packed, place_ref, x_ref, *refs):
    if packed is None:
        w_ref, gi_ref, gq_ref, gk_ref, cos_ref, sin_ref, q_ref, k_ref, v_ref, s_ref, n_ref = refs
    else:
        own_ref, other_ref, gi_ref, gq_ref, gk_ref, cos_ref, sin_ref, q_ref, k_ref, v_ref, s_ref, n_ref, w_ref = refs

        @pl.when(pl.program_id(0) == 0)
        def _():
            pack_qkv(place_ref, own_ref, other_ref, w_ref, *packed)

    x = x_ref[...].astype(F32)
    normed = (x * inv_rms(x) * gi_ref[...]).astype(BF)
    n_ref[...] = normed
    cos = cos_ref[...]
    sin = sin_ref[...]
    width = HEADS * HEAD_DIM
    v_ref[...] = dot_nt(normed, w_ref[width + HEAD_DIM :, :]).astype(BF)
    lane = lax.broadcasted_iota(jnp.int32, s_ref.shape, 1)
    saved = jnp.zeros(s_ref.shape, F32)
    for h in range(HEADS + 1):
        raw = dot_nt(normed, w_ref[h * HEAD_DIM : (h + 1) * HEAD_DIM, :])
        inv = inv_rms(raw)
        saved = jnp.where(lane == h, inv, saved)
        gain = gq_ref[...] * QUERY_SCALE if h < HEADS else gk_ref[...]
        y = raw * inv * gain
        y1 = y[:, :HALF]
        y2 = y[:, HALF:]
        out = q_ref.at[h] if h < HEADS else k_ref
        out[:, :HALF] = (y1 * cos - y2 * sin).astype(BF)
        out[:, HALF:] = (y2 * cos + y1 * sin).astype(BF)
    s_ref[...] = saved


def qkv_call(place, x, weights, packed, gi, gq, gk, cos, sin):
    rows, d = x.shape
    b = ROW_BLOCK
    width = HEADS * HEAD_DIM
    row = lambda n: pl.BlockSpec((b, n), lambda i, *_: (i, 0))
    sds = jax.ShapeDtypeStruct
    whole = sds((width + 2 * HEAD_DIM, d), BF)
    outs = [sds((HEADS, rows, HEAD_DIM), BF), sds((rows, HEAD_DIM), BF), sds((rows, HEAD_DIM), BF),
            sds((rows, 128), F32), sds((rows, d), BF)]
    out_specs = [pl.BlockSpec((HEADS, b, HEAD_DIM), lambda i, *_: (0, i, 0)), row(HEAD_DIM), row(HEAD_DIM), row(128),
                 row(d)]
    if packed is not None:
        outs.append(whole)
        out_specs.append(pl.BlockSpec(whole.shape, lambda i, *_: (0, 0)))
    result = pl.pallas_call(
        functools.partial(qkv_kernel, packed),
        grid_spec=pltpu.PrefetchScalarGridSpec(
            num_scalar_prefetch=1,
            grid=(rows // b,),
            in_specs=[row(d)] + [const_spec(w.shape) for w in weights]
            + [const_spec((1, d)), const_spec((1, HEAD_DIM)), const_spec((1, HEAD_DIM)), row(HALF), row(HALF)],
            out_specs=out_specs,
        ),
        out_shape=outs,
        compiler_params=params(),
        cost_estimate=cost(2 * rows * d * (width + 2 * HEAD_DIM), 12 * rows * d),
        name="qkv_rows",
    )(place, x, *weights, gi, gq, gk, cos, sin)
    return result if packed is not None else list(result) + [weights[0]]


def attend_kernel(blocks, first_ref, q_ref, k_ref, v_ref, start_ref, p_ref, o_ref):
    i = pl.program_id(0)
    qb = lax.rem(i, blocks)
    first = first_ref[i]
    count = qb + 1 - first
    m_rows = HEADS * QBLOCK
    for n in range(1, blocks + 1):

        @pl.when(count == n)
        def _():
            base = pl.multiple_of(first * QBLOCK, QBLOCK)
            window = pl.ds(base, n * QBLOCK)
            q = q_ref[...].reshape(m_rows, HEAD_DIM)
            scores = dot_nt(q, k_ref[window, :])
            col = lax.broadcasted_iota(jnp.int32, scores.shape, 1) + base
            row = lax.broadcasted_iota(jnp.int32, (QBLOCK, 1), 0) + qb * QBLOCK
            row = jnp.concatenate([row] * HEADS, axis=0)
            start = jnp.concatenate([start_ref[...]] * HEADS, axis=0)
            scores = jnp.where((col >= start) & (col <= row), scores, NEG_FILL)
            e = jnp.exp(scores - jnp.max(scores, axis=-1, keepdims=True))
            probs = (e * (1.0 / jnp.sum(e, axis=-1, keepdims=True))).astype(BF)
            p_ref[0, :, : n * QBLOCK] = probs
            out = dot_nn(probs, v_ref[window, :]).astype(BF)
            for h in range(HEADS):
                o_ref[:, h * HEAD_DIM : (h + 1) * HEAD_DIM] = out[h * QBLOCK : (h + 1) * QBLOCK]


def attend_call(first, q, k, v, start, slots):
    rows = k.shape[0]
    slot_rows = rows // slots
    blocks = slot_rows // QBLOCK
    width = HEADS * HEAD_DIM
    slot = pl.BlockSpec((slot_rows, HEAD_DIM), lambda i, *_: (i // blocks, 0))
    return pl.pallas_call(
        functools.partial(attend_kernel, blocks),
        grid_spec=pltpu.PrefetchScalarGridSpec(
            num_scalar_prefetch=1,
            grid=(slots * blocks,),
            in_specs=[pl.BlockSpec((HEADS, QBLOCK, HEAD_DIM), lambda i, *_: (0, i, 0)), slot, slot,
                      pl.BlockSpec((QBLOCK, 1), lambda i, *_: (i, 0))],
            out_specs=[pl.BlockSpec((1, HEADS * QBLOCK, slot_rows), lambda i, *_: (i, 0, 0)),
                       pl.BlockSpec((QBLOCK, width), lambda i, *_: (i, 0))],
        ),
        out_shape=[jax.ShapeDtypeStruct((slots * blocks, HEADS * QBLOCK, slot_rows), BF),
                   jax.ShapeDtypeStruct((rows, width), BF)],
        compiler_params=params(),
        cost_estimate=cost(4 * rows * slot_rows * width * 5 // 8, 2 * rows * slot_rows * HEADS + 8 * rows * width,
                           rows * slot_rows * HEADS * 5 // 8),
        name="attend_rows",
    )(first, q, k, v, start)


def load_weights(place_ref, srcs, wo_s, wg_s, wu_s, wd_s, sem, nf, nq):
    b_own, b_other, c_own, c_other = srcs
    half = b_own.shape[0]
    copies = []
    for n, (b, c) in enumerate(((b_own, c_own), (b_other, c_other))):
        to = pl.ds(n * half, half)
        copies.append(pltpu.make_async_copy(b.at[:, pl.ds(0, nf), :], wg_s.at[to], sem.at[3 * n]))
        copies.append(pltpu.make_async_copy(b.at[:, pl.ds(nf, nf), :], wu_s.at[to], sem.at[3 * n + 1]))
        copies.append(pltpu.make_async_copy(c, wd_s.at[to], sem.at[3 * n + 2]))
    copies.append(pltpu.make_async_copy(b_own.at[:, pl.ds(2 * nf, nq), :], wo_s.at[pl.ds(0, half)], sem.at[6]))
    copies.append(pltpu.make_async_copy(b_other.at[:, pl.ds(2 * nf, nq), :], wo_s.at[pl.ds(half, half)], sem.at[7]))
    return copies


def ffn_kernel(slot_rows, packed, total_ref, place_ref, a_ref, x_ref, og_ref, *refs):
    if packed is None:
        wo_ref, wg_ref, wu_ref, wd_ref = refs[:4]
        refs = refs[4:]
    else:
        srcs = refs[:4]
        wo_ref, wo_s, wg_s, wu_s, wd_s, sem = refs[-6:]
        refs = refs[4:-6]
        flat = lambda r: r.reshape(r.shape[0] * r.shape[1], r.shape[2])
        wg_ref, wu_ref, wd_ref = flat(wg_s), flat(wu_s), flat(wd_s)
        copies = load_weights(place_ref, srcs, wo_s, wg_s, wu_s, wd_s, sem, *packed)

        @pl.when(pl.program_id(0) == 0)
        def _():
            for copy in copies[::-1]:
                copy.start()
            copies[7].wait()
            copies[6].wait()
            nq = packed[1]
            for j in range(wo_s.shape[0]):
                wo_ref[j * nq : (j + 1) * nq, :] = wo_s[place_ref[j]]
            for copy in copies[:6]:
                copy.wait()

    (ga_ref, gf_ref, go_ref, out_ref, wide_ref, fin_ref, gfo_ref, gb_ref, gatt_ref, gm_ref, dg_ref,
     gate_s, up_s) = refs
    i = pl.program_id(0)
    b = x_ref.shape[0]
    ff = wg_ref.shape[0]

    @pl.when(i == 0)
    def _():
        dg_ref[...] = jnp.zeros_like(dg_ref)

    branch = dot_nn(a_ref[...], wo_ref[...])
    s_b = inv_rms(branch)
    nb = branch * s_b
    middle = x_ref[...].astype(F32) + nb * ga_ref[...]
    s_m = inv_rms(middle)
    nm = middle * s_m
    ffn_in = (nm * gf_ref[...]).astype(BF)
    fin_ref[...] = ffn_in

    gate_s[...] = dot_nt(ffn_in, wg_ref[...])
    up_s[...] = dot_nt(ffn_in, wu_ref[...])
    gate = gate_s[...]
    t = jnp.tanh(gate * (GELU_C + (GELU_C * GELU_A) * (gate * gate)))
    hidden = (0.5 * gate * (1.0 + t) * up_s[...]).astype(BF)
    wide_ref[:, 2 * ff :] = hidden
    ffn_out = dot_nn(hidden, wd_ref[...])
    s_f = inv_rms(ffn_out)
    nf = ffn_out * s_f
    out_ref[...] = (middle + nf * go_ref[...]).astype(BF)

    per_slot = slot_rows // b
    row = lax.broadcasted_iota(jnp.int32, (b, 1), 0) + lax.rem(i, per_slot) * b
    live = row < total_ref[i // per_slot]
    upstream = jnp.where(live, og_ref[...].astype(F32), 0.0)
    dg_fo = row_sum(upstream * nf)
    scaled = upstream * go_ref[...]
    gfo = (s_f * (scaled - nf * jnp.mean(scaled * nf, axis=-1, keepdims=True))).astype(BF)
    gfo_ref[...] = gfo
    gh = dot_nt(gfo, wd_ref[...])
    gate = gate_s[...]
    sq = gate * gate
    t = jnp.tanh(gate * (GELU_C + (GELU_C * GELU_A) * sq))
    half_t = 0.5 + 0.5 * t
    slope = half_t + (0.5 * gate) * (1.0 - t * t) * (GELU_C + (3.0 * GELU_C * GELU_A) * sq)
    gg = (gh * up_s[...] * slope).astype(BF)
    gu = (gh * (gate * half_t)).astype(BF)
    wide_ref[:, :ff] = gg
    wide_ref[:, ff : 2 * ff] = gu
    gfin = dot_nn(gg, wg_ref[...]) + dot_nn(gu, wu_ref[...])
    dg_fi = row_sum(gfin * nm)
    scaled = gfin * gf_ref[...]
    gm = upstream + s_m * (scaled - nm * jnp.mean(scaled * nm, axis=-1, keepdims=True))
    gm_ref[...] = gm
    dg_at = row_sum(gm * nb)
    scaled = gm * ga_ref[...]
    gb = (s_b * (scaled - nb * jnp.mean(scaled * nb, axis=-1, keepdims=True))).astype(BF)
    gb_ref[...] = gb
    gatt_ref[...] = dot_nt(gb, wo_ref[...]).astype(BF)
    dg_ref[0:1, :] += dg_fo
    dg_ref[1:2, :] += dg_fi
    dg_ref[2:3, :] += dg_at


def ffn_call(total, place, attended, x, og, weights, packed, ff, ga, gf, go, slots):
    rows, d = x.shape
    width = attended.shape[1]
    b = FFN_ROWS
    row = lambda n: pl.BlockSpec((b, n), lambda i, *_: (i, 0))
    vec = const_spec((1, d))
    sds = jax.ShapeDtypeStruct
    scratch = [pltpu.VMEM((b, ff), F32), pltpu.VMEM((b, ff), F32)]
    if packed is None:
        weight_specs = [const_spec(w.shape) for w in weights]
    else:
        nf, nq = packed
        weight_specs = [pl.BlockSpec(memory_space=pl.ANY)] * 4
        scratch += [pltpu.VMEM((width, d), BF), pltpu.VMEM((width // nq, nq, d), BF)]
        scratch += [pltpu.VMEM((ff // nf, nf, d), BF)] * 3 + [pltpu.SemaphoreType.DMA((8,))]
    return pl.pallas_call(
        functools.partial(ffn_kernel, rows // slots, packed),
        grid_spec=pltpu.PrefetchScalarGridSpec(
            num_scalar_prefetch=2,
            grid=(rows // b,),
            in_specs=[row(width), row(d), row(d)] + weight_specs + [vec, vec, vec],
            out_specs=[row(d), row(3 * ff), row(d), row(d), row(d), row(width), row(d),
                       pl.BlockSpec((8, d), lambda i, *_: (0, 0))],
            scratch_shapes=scratch,
        ),
        out_shape=[sds((rows, d), BF), sds((rows, 3 * ff), BF), sds((rows, d), BF), sds((rows, d), BF),
                   sds((rows, d), BF), sds((rows, width), BF), sds((rows, d), F32), sds((8, d), F32)],
        compiler_params=params(),
        cost_estimate=cost(4 * rows * d * (width + 3 * ff), rows * (6 * ff + 12 * d), 2 * rows * ff),
        name="ffn_rows",
    )(total, place, attended, x, og, *weights, ga, gf, go)


def wide_grad_kernel(chunks, left_ref, r_ref, own_ref, other_ref):
    grads = dot_tn(left_ref[...], r_ref[...]).astype(BF).reshape(own_ref.shape)
    own = lax.rem(pl.program_id(0), chunks) < chunks // 2

    @pl.when(own)
    def _():
        own_ref[...] = grads

    @pl.when(jnp.logical_not(own))
    def _():
        other_ref[...] = grads


def wide_grad_call(wide, begin, many, right, ff, nf, total):
    rows, d = right.shape
    chunks = ff // FF_BLOCK
    half = ff // nf // 2
    last = chunks // 2 - 1
    out = jax.ShapeDtypeStruct((half, total, d), BF)
    block = (FF_BLOCK // nf, nf, d)
    return pl.pallas_call(
        functools.partial(wide_grad_kernel, chunks),
        grid=(chunks * many,),
        in_specs=[pl.BlockSpec((rows, FF_BLOCK), lambda i: (0, begin * chunks + i)), const_spec(right.shape)],
        out_specs=[pl.BlockSpec(block, lambda i: (jnp.minimum(lax.rem(i, chunks), last), i // chunks, 0)),
                   pl.BlockSpec(block, lambda i: (jnp.maximum(lax.rem(i, chunks) - last - 1, 0), i // chunks, 0))],
        out_shape=[out, out],
        compiler_params=params(),
        cost_estimate=cost(2 * rows * ff * many * d, 2 * rows * ff * many),
        name="wide_grads",
    )(wide, right)


def out_grad_kernel(owner_ref, a_ref, r_ref, before_own, before_other, own_ref, other_ref, sum_s):
    half, nq, d = own_ref.shape
    sum_s[...] = dot_tn(a_ref[...], r_ref[...])
    for j in range(2 * half):
        rows = sum_s[pl.ds(pl.multiple_of(owner_ref[j] * nq, nq), nq), :].astype(BF)
        if j < half:
            own_ref[j] = rows
        else:
            other_ref[j - half] = rows


def out_grad_call(owner, attended, gb, before, nq):
    rows, width = attended.shape
    half, total, d = before[0].shape
    place = pl.BlockSpec((half, nq, d), lambda i, *_: (0, total // nq - 1, 0))
    return pl.pallas_call(
        out_grad_kernel,
        grid_spec=pltpu.PrefetchScalarGridSpec(
            num_scalar_prefetch=1,
            grid=(1,),
            in_specs=[const_spec(attended.shape), const_spec(gb.shape), pl.BlockSpec(memory_space=pl.ANY),
                      pl.BlockSpec(memory_space=pl.ANY)],
            out_specs=[place, place],
            scratch_shapes=[pltpu.VMEM((width, d), F32)],
        ),
        out_shape=[jax.ShapeDtypeStruct(before[0].shape, BF)] * 2,
        input_output_aliases={3: 0, 4: 1},
        compiler_params=params(),
        cost_estimate=cost(2 * rows * width * d, 2 * rows * width),
        name="out_grads",
    )(owner, attended, gb, *before)


def qkv_grad_kernel(owner_ref, gq_ref, gk_ref, gv_ref, n_ref, w_ref, gi_ref, own_ref, other_ref, dg_ref, sum_s):
    i = pl.program_id(0)
    half, total, d = own_ref.shape
    nk = HEAD_DIM // (2 * half)
    nq = total - 2 * nk
    step = gq_ref.shape[1]
    width = HEADS * HEAD_DIM
    last = width // step

    @pl.when(i < last)
    def _():
        sum_s[pl.ds(pl.multiple_of(i * step, step), step), :] = dot_tn(gq_ref[...], n_ref[...])

    @pl.when(i == last)
    def _():
        sum_s[width:, :] = dot_tn(jnp.concatenate([gk_ref[...], gv_ref[...]], axis=1), n_ref[...])
        dg = row_sum(sum_s[...] * w_ref[...].astype(F32)) / gi_ref[...]
        dg_ref[...] = jnp.broadcast_to(dg, dg_ref.shape)
        for j in range(2 * half):
            at = owner_ref[j]
            block = jnp.concatenate(
                [
                    sum_s[pl.ds(pl.multiple_of(at * nq, nq), nq), :],
                    sum_s[pl.ds(pl.multiple_of(width + at * nk, nk), nk), :],
                    sum_s[pl.ds(pl.multiple_of(width + HEAD_DIM + at * nk, nk), nk), :],
                ],
                axis=0,
            ).astype(BF)
            if j < half:
                own_ref[j] = block
            else:
                other_ref[j - half] = block


def qkv_grad_call(owner, gq, gk, gv, normed, w_qkv, gi, total):
    rows, d = normed.shape
    half = owner.shape[0] // 2
    step = 2 * HEAD_DIM
    last = HEADS * HEAD_DIM // step
    out = pl.BlockSpec((half, total, d), lambda i, *_: (0, 0, 0))
    return pl.pallas_call(
        qkv_grad_kernel,
        grid_spec=pltpu.PrefetchScalarGridSpec(
            num_scalar_prefetch=1,
            grid=(last + 1,),
            in_specs=[pl.BlockSpec((rows, step), lambda i, *_: (0, jnp.minimum(i, last - 1))),
                      const_spec(gk.shape), const_spec(gv.shape), const_spec(normed.shape), const_spec(w_qkv.shape),
                      const_spec(gi.shape)],
            out_specs=[out, out, pl.BlockSpec((8, d), lambda i, *_: (0, 0))],
            scratch_shapes=[pltpu.VMEM(((HEADS + 2) * HEAD_DIM, d), F32)],
        ),
        out_shape=[jax.ShapeDtypeStruct((half, total, d), BF)] * 2 + [jax.ShapeDtypeStruct((8, d), F32)],
        compiler_params=params(),
        cost_estimate=cost(2 * rows * d * (HEADS + 2) * HEAD_DIM, 4 * rows * HEADS * HEAD_DIM),
        name="qkv_grads",
    )(owner, gq, gk, gv, normed, w_qkv, gi)


def rope_back_halves(g1, g2, cos, sin):
    return g1 * cos + g2 * sin, g2 * cos - g1 * sin


def norm_rope_back(grad, rotated, inv, gain, cos, sin, scale):
    m = jnp.mean(grad * rotated, axis=-1, keepdims=True)
    dy1, dy2 = rope_back_halves(grad[:, :HALF], grad[:, HALF:], cos, sin)
    u1, u2 = rope_back_halves(rotated[:, :HALF], rotated[:, HALF:], cos, sin)
    dy = jnp.concatenate([dy1, dy2], axis=1) * scale
    n = jnp.concatenate([u1, u2], axis=1) * ((1.0 / scale) / gain)
    return inv * (dy * gain - n * m), row_sum(dy * n)


def attend_back_kernel(blocks, offset, kept, first_ref, p_ref, q_ref, k_ref, v_ref, do_ref, s_ref, cos_ref, sin_ref,
                       gq_ref, gk_ref, *rest):
    gqr_ref, gkr_ref, gv_ref, dg_ref, dq_s, dk_s, dv_s = rest[kept:]
    i = pl.program_id(0)
    qb = i
    first = first_ref[offset + i]
    count = qb + 1 - first
    m_rows = HEADS * QBLOCK

    @pl.when(i == 0)
    def _():
        dg_ref[...] = jnp.zeros_like(dg_ref)

    @pl.when(qb == 0)
    def _():
        dk_s[...] = jnp.zeros_like(dk_s)
        dv_s[...] = jnp.zeros_like(dv_s)

    for n in range(1, blocks + 1):

        @pl.when(count == n)
        def _():
            base = pl.multiple_of(first * QBLOCK, QBLOCK)
            window = pl.ds(base, n * QBLOCK)
            do = jnp.concatenate([do_ref[:, h * HEAD_DIM : (h + 1) * HEAD_DIM] for h in range(HEADS)], axis=0)
            q = q_ref[...].reshape(m_rows, HEAD_DIM)
            probs = p_ref[0, :, : n * QBLOCK]
            dp = dot_nt(do, v_ref[window, :])
            pf = probs.astype(F32)
            total = jnp.sum(pf * dp, axis=-1, keepdims=True)
            ds = (pf * (dp - total)).astype(BF)
            dq_s[...] = dot_nn(ds, k_ref[window, :])
            dk_s[window, :] += dot_tn(ds, q)
            dv_s[window, :] += dot_tn(probs, do)

    rows = pl.ds(pl.multiple_of(qb * QBLOCK, QBLOCK), QBLOCK)
    cos = cos_ref[rows, :]
    sin = sin_ref[rows, :]
    inv = s_ref[rows, :]
    for h in range(HEADS):
        grad, dg = norm_rope_back(dq_s[h * QBLOCK : (h + 1) * QBLOCK, :], q_ref[h].astype(F32), inv[:, h : h + 1],
                                  gq_ref[...], cos, sin, QUERY_SCALE)
        gqr_ref[:, h * HEAD_DIM : (h + 1) * HEAD_DIM] = grad.astype(BF)
        dg_ref[0:1, :] += dg

    @pl.when(qb == blocks - 1)
    def _():
        gv_ref[...] = dv_s[...].astype(BF)
        grad, dg = norm_rope_back(dk_s[...], k_ref[...].astype(F32), s_ref[:, HEADS : HEADS + 1], gk_ref[...],
                                  cos_ref[...], sin_ref[...], 1.0)
        gkr_ref[...] = grad.astype(BF)
        dg_ref[1:2, :] += dg


def attend_back_call(first, p, q, k, v, do, s, cos, sin, gq, gk, slots, which, previous):
    rows = k.shape[0]
    slot_rows = rows // slots
    blocks = slot_rows // QBLOCK
    width = HEADS * HEAD_DIM
    base = which * blocks
    slot = lambda n: pl.BlockSpec((slot_rows, n), lambda i, *_: (which, 0))
    block = lambda n: pl.BlockSpec((QBLOCK, n), lambda i, *_: (base + i, 0))
    sds = jax.ShapeDtypeStruct
    kept = () if previous is None else tuple(previous)
    return pl.pallas_call(
        functools.partial(attend_back_kernel, blocks, base, len(kept)),
        grid_spec=pltpu.PrefetchScalarGridSpec(
            num_scalar_prefetch=1,
            grid=(blocks,),
            in_specs=[pl.BlockSpec((1, HEADS * QBLOCK, slot_rows), lambda i, *_: (base + i, 0, 0)),
                      pl.BlockSpec((HEADS, QBLOCK, HEAD_DIM), lambda i, *_: (0, base + i, 0)),
                      slot(HEAD_DIM), slot(HEAD_DIM), block(width), slot(128), slot(HALF), slot(HALF),
                      const_spec((1, HEAD_DIM)), const_spec((1, HEAD_DIM))]
            + [pl.BlockSpec(memory_space=pl.ANY)] * len(kept),
            out_specs=[block(width), slot(HEAD_DIM), slot(HEAD_DIM), pl.BlockSpec((8, HEAD_DIM), lambda i, *_: (0, 0))],
            scratch_shapes=[pltpu.VMEM((HEADS * QBLOCK, HEAD_DIM), F32), pltpu.VMEM((slot_rows, HEAD_DIM), F32),
                            pltpu.VMEM((slot_rows, HEAD_DIM), F32)],
        ),
        out_shape=[sds((rows, width), BF), sds((rows, HEAD_DIM), BF), sds((rows, HEAD_DIM), BF),
                   sds((8, HEAD_DIM), F32)],
        input_output_aliases={11 + j: j for j in range(len(kept))},
        compiler_params=params(),
        cost_estimate=cost(8 * slot_rows * slot_rows * width * 5 // 8,
                           2 * slot_rows * slot_rows * HEADS + 12 * slot_rows * width),
        name="attend_back_rows",
    )(first, p, q, k, v, do, s, cos, sin, gq, gk, *kept)


def input_back_kernel(gq_ref, gk_ref, gv_ref, x_ref, gm_ref, w_ref, gi_ref, gx_ref):
    width = HEADS * HEAD_DIM
    gn = dot_nn(gq_ref[...], w_ref[:width, :])
    gn += dot_nn(gk_ref[...], w_ref[width : width + HEAD_DIM, :])
    gn += dot_nn(gv_ref[...], w_ref[width + HEAD_DIM :, :])
    x = x_ref[...].astype(F32)
    inv = inv_rms(x)
    n = x * inv
    scaled = gn * gi_ref[...]
    gx = inv * (scaled - n * jnp.mean(scaled * n, axis=-1, keepdims=True))
    gx_ref[...] = (gm_ref[...] + gx).astype(BF)


def input_back_call(gq, gk, gv, x, gm, w_qkv, gi):
    rows, d = x.shape
    b = ROW_BLOCK
    row = lambda n: pl.BlockSpec((b, n), lambda i: (i, 0))
    return pl.pallas_call(
        input_back_kernel,
        grid=(rows // b,),
        in_specs=[row(gq.shape[1]), row(HEAD_DIM), row(HEAD_DIM), row(d), row(d), const_spec(w_qkv.shape),
                  const_spec((1, d))],
        out_specs=row(d),
        out_shape=jax.ShapeDtypeStruct((rows, d), BF),
        compiler_params=params(),
        cost_estimate=cost(2 * rows * d * w_qkv.shape[0], 14 * rows * d),
        name="input_back_rows",
    )(gq, gk, gv, x, gm, w_qkv, gi)


def level_list(count):
    levels = [(1, 2)]
    stride = 2
    while stride < count:
        size = 4 if count // stride >= 4 else 2
        levels.append((stride, size))
        stride *= size
    return levels


def send(x, count, offset):
    return lax.ppermute(x, "fsdp", [(i, i ^ offset) for i in range(count)])


def swap(x, count, level):
    stride, size = level
    return [send(x, count, k * stride) for k in range(1, size)]


def block_offsets(count):
    offsets = [0]
    for stride, size in level_list(count)[::-1]:
        offsets = [o ^ (k * stride) for k in range(size) for o in offsets]
    return offsets


def tie(values, *after):
    return lax.optimization_barrier((values, after))[0]


def open_blocks(x, levels):
    return x.reshape((1,) * len(levels) + x.shape)


def join(own, received, axis):
    return jnp.concatenate([own] + list(received), axis=axis)


def part(g, axis, k):
    return lax.slice_in_dim(g, k, k + 1, axis=axis)


def give(g, count, level, axis):
    stride, size = level
    return [send(part(g, axis, k).astype(BF), count, k * stride) for k in range(1, size)]


def add_up(g, received, axis, kind=BF):
    total = part(g, axis, 0).astype(F32)
    for r in received:
        total = total + r.astype(F32)
    return total.astype(kind)


def slot_layout(lengths, row_count):
    seq_ends = jnp.cumsum(lengths, axis=1, dtype=jnp.int32)
    rows = lax.broadcasted_iota(jnp.int32, (lengths.shape[0], row_count), 1)
    passed = rows[:, :, None] >= seq_ends[:, None, :]
    start = jnp.sum(jnp.where(passed, lengths[:, None, :], 0), axis=2, dtype=jnp.int32)
    return start, rows - start, seq_ends[:, -1]


def shards(count, tokens, out_grad, seq_lengths, w_query, w_key, w_value, w_output, w_gate, w_up, w_down,
           gain_input, gain_query, gain_key, gain_attn, gain_ffn_in, gain_ffn_out):
    slots = seq_lengths.shape[0]
    rows, d = tokens.shape
    slot_rows = rows // slots
    me = lax.axis_index("fsdp")
    levels = level_list(count)
    depth = len(levels)
    core, near, far = levels[0], levels[1], levels[2:]
    order = block_offsets(count)
    inverse = [0] * count
    for j, o in enumerate(order):
        inverse[o] = j
    place = jnp.array(inverse, jnp.int32)[jnp.arange(count, dtype=jnp.int32) ^ me]
    owner = jnp.array(order, jnp.int32) ^ me
    nq, nk, nf = w_query.shape[1], w_key.shape[1], w_gate.shape[1]

    aligned = nq % 16 == 0 and nk == 8 and nf % 16 == 0
    na = nq + 2 * nk

    a = open_blocks(jnp.concatenate([w_query.T, w_key.T, w_value.T], axis=0), levels)
    b = open_blocks(jnp.concatenate([w_gate.T, w_up.T, w_output.T], axis=0), levels)
    c = open_blocks(w_down.T, levels)
    start, position, total = slot_layout(seq_lengths, slot_rows)

    for n in range(depth - 1, 1, -1):
        a = join(a, swap(a, count, levels[n]), n)
    c = join(c, swap(c, count, near), 1)
    for n in range(depth - 1, 1, -1):
        b = join(b, swap(b, count, levels[n]), n)
    inv_freq = jnp.exp(lax.iota(jnp.int32, HALF).astype(F32) * (-2.0 * math.log(ROPE_BASE) / HEAD_DIM))
    phases = position.reshape(rows, 1).astype(F32) * inv_freq[None, :]
    received = swap(a, count, near)
    cos = jnp.cos(phases)
    sin = jnp.sin(phases)
    received, cos, sin = lax.optimization_barrier((received, cos, sin))
    a = join(a, received, 1)
    b = tie(b, a, c)
    b_near = swap(b, count, near)
    a_core = swap(a, count, core)[0]
    half = count // 2
    a, a_core = a.reshape((half, na, d)), a_core.reshape((half, na, d))
    first = (start[:, ::QBLOCK] // QBLOCK).reshape(-1)
    start_col = start.reshape(rows, 1)
    gi, gq, gk = gain_input[None], gain_query[None], gain_key[None]
    if aligned:
        a_weights, a_packed = (a, a_core), (nq, nk)
    else:
        a = jnp.concatenate([a, a_core], axis=0)[place]
        w_qkv = jnp.concatenate(
            [a[:, :nq].reshape(-1, d), a[:, nq : nq + nk].reshape(-1, d), a[:, nq + nk :].reshape(-1, d)], axis=0
        )
        a_weights, a_packed = (w_qkv,), None

    a_weights, b = lax.optimization_barrier((a_weights, b))
    for n in range(2, depth - 1):
        c = join(c, swap(c, count, levels[n]), n)
    c_far, c_late = [], []
    if depth > 2:
        stride, size = levels[-1]
        early = tie(c, b)
        c_far = [send(early, count, step * stride) for step in range(1, min(size, 3))]
    q, k, v, s, normed, w_qkv = qkv_call(place, tokens, a_weights, a_packed, gi, gq, gk, cos, sin)
    if depth > 2:
        q, late = lax.optimization_barrier((q, c))
        c_late = [send(late, count, step * stride) for step in range(3, size)]
    p, attended = attend_call(first, q, k, v, start_col, slots)

    b_near, c_far = tie((b_near, c_far + c_late), attended)
    b = join(b, b_near, 1)
    b_core = swap(b, count, core)[0]
    c = join(c, c_far, depth - 1)
    c_core = swap(c, count, core)[0]
    b, b_core = b.reshape((half, 2 * nf + nq, d)), b_core.reshape((half, 2 * nf + nq, d))
    c, c_core = c.reshape((half, nf, d)), c_core.reshape((half, nf, d))
    if aligned:
        b_weights, b_packed = (b, b_core, c, c_core), (nf, nq)
    else:
        b = jnp.concatenate([b, b_core], axis=0)
        b_weights = (b[:, 2 * nf :][place].reshape(-1, d), b[:, :nf].reshape(-1, d), b[:, nf : 2 * nf].reshape(-1, d),
                     jnp.concatenate([c, c_core], axis=0).reshape(-1, d))
        b_packed = None
    out, wide, fin, gfo, gb, gatt, gm, dg_ffn = ffn_call(
        total, place, attended, tokens, out_grad, b_weights, b_packed, count * nf, gain_attn[None],
        gain_ffn_in[None], gain_ffn_out[None], slots
    )

    sizes = tuple(size for _, size in levels[1:])
    spread = lambda g: g.reshape(sizes + g.shape[1:])
    halves = lambda g: (g[:half], g[half:])
    if aligned:
        gb_pair = wide_grad_call(wide, 0, 2, fin, count * nf, nf, 2 * nf + nq)
        gb_pair = out_grad_call(owner, attended, gb, gb_pair, nq)
    else:
        g_out = dot_tn(attended, gb).astype(BF).reshape(count, nq, d)[owner]
        g_wide = wide_grad_call(wide, 0, 2, fin, count * nf, nf, 2 * nf)
        gb_pair = [jnp.concatenate(both, axis=1) for both in zip(g_wide, halves(g_out))]
    gb_all, gb_other = gb_pair
    stride, size = near
    gb_core = send(gb_other, count, core[0])
    gc_all, gc_other = wide_grad_call(wide, 2, 1, tie(gfo, gb_other), count * nf, nf, nf)
    gb_core = tie(gb_core, gc_all)
    gb_all = spread((gb_all.astype(F32) + gb_core.astype(F32)).astype(BF))
    ask = lambda k: send(part(gb_all, 0, k), count, k * stride)
    gb_near = [ask(k) for k in range(1, min(size, 3))]
    gc_core = send(gc_other, count, core[0])

    p = tie(p, gb_all)
    back = None
    dg_att = 0.0
    for which in range(slots):
        back = attend_back_call(first, p, q, k, v, gatt, s, cos, sin, gq, gk, slots, which, back)
        dg_att = dg_att + back[3]
        back = back[:3]
        if which == 0:
            gb_near, gc_core = tie((gb_near, gc_core), back[0])
            gc_all = spread((gc_all.astype(F32) + gc_core.astype(F32)).astype(BF))
            back = tie(back, gb_near, gc_all)
            gc_far, gc_late = [], []
            if depth > 2:
                give_c = lambda g, step: send(part(g, depth - 2, step), count, step * levels[-1][0])
                gc_far = [give_c(gc_all, step) for step in range(1, min(levels[-1][1], 3))]
            gb_all = tie(gb_all, gb_near, gc_all)
            gb_last = [ask(k) for k in range(3, size)]
    back, gb_last, gc_far, gc_rest = lax.optimization_barrier((back, gb_last, gc_far, gc_all))
    gqr, gkr, gv = back
    if depth > 2:
        gc_late = [give_c(gc_rest, step) for step in range(3, levels[-1][1])]
    if aligned:
        ga_all, ga_other, dg_in = qkv_grad_call(owner, gqr, gkr, gv, normed, w_qkv, gi, na)
    else:
        wg = lambda left, n: dot_tn(left, normed).astype(BF)
        whole = [wg(gqr, nq), wg(gkr, nk), wg(gv, nk)]
        dg_in = jnp.sum(jnp.concatenate(whole, axis=0).astype(F32) * w_qkv.astype(F32), axis=0, keepdims=True) / gi
        whole = [g.reshape(count, -1, d) for g in whole]
        ga_all, ga_other = halves(jnp.concatenate(whole, axis=1)[owner])
    gains = jnp.concatenate([dg_in[0], dg_att[0], dg_att[1], dg_ffn[2], dg_ffn[1], dg_ffn[0]])
    gains = jnp.pad(gains, (0, -gains.shape[0] % d)).reshape(-1, d)
    n_gain = gains.shape[0]

    def with_gains(g):
        high = gains.astype(BF)
        low = (gains - high.astype(F32)).astype(BF)
        return jnp.concatenate([g.astype(BF).reshape(-1, d), high, low], axis=0)

    def split_gains(message, shape):
        rest = message[-2 * n_gain :].astype(F32)
        return message[: -2 * n_gain].reshape(shape).astype(F32), rest[:n_gain] + rest[n_gain:]

    ga_core = send(with_gains(ga_other), count, core[0])
    gb_last = tie(gb_last, ga_other)
    gb_all = add_up(gb_all, gb_near + gb_last, 0)
    ga_core, gb_all = lax.optimization_barrier((ga_core, gb_all))
    received, more = split_gains(ga_core, ga_all.shape)
    ga_all = spread(ga_all.astype(F32) + received)
    gains = gains + more
    gb_late = []
    for n in range(1, depth):
        stride, size = levels[n]
        pieces = [part(ga_all, n - 1, step) for step in range(size)]
        messages = [send(with_gains(piece), count, step * stride) for step, piece in enumerate(pieces) if step]
        if n == 1:
            if depth > 2:
                far_stride, far_size = levels[2]
                give_far = lambda step: send(part(gb_all, 1, step), count, step * far_stride)
                gb_late = [give_far(step) for step in range(1, min(far_size, 3))]
            gm = tie(gm, ga_all, gb_all)
            grad_tokens = input_back_call(gqr, gkr, gv, tokens, gm, w_qkv, gi)
            messages, gb_late, gb_rest, gc_all, gc_late = tie((messages, gb_late, gb_all, gc_all, gc_late), grad_tokens)
            if depth > 2:
                gc_all = add_up(gc_all, gc_far + gc_late, depth - 2)
            if depth > 2:
                gb_late = gb_late + [send(part(gb_rest, 1, step), count, step * far_stride)
                                     for step in range(3, far_size)]
        ga_all = pieces[0]
        for message in messages:
            received, more = split_gains(message, ga_all.shape)
            ga_all = ga_all + received
            gains = gains + more
    for n in range(2, depth):
        received = gb_late if n == 2 else give(gb_all, count, levels[n], n - 1)
        gb_all = add_up(gb_all, received, n - 1, F32 if n == depth - 1 else BF)
    for n in range(depth - 2, 0, -1):
        gc_all = add_up(gc_all, give(gc_all, count, levels[n], n - 1), n - 1, F32 if n == 1 else BF)
    g_qkv = ga_all.reshape(nq + 2 * nk, d).astype(F32)
    g_b = gb_all.reshape(2 * nf + nq, d).astype(F32)
    g_c = gc_all.reshape(nf, d).astype(F32)
    gains = gains.reshape(-1)
    h = HEAD_DIM
    return (
        out,
        grad_tokens,
        g_qkv[:nq].T,
        g_qkv[nq : nq + nk].T,
        g_qkv[nq + nk :].T,
        g_b[2 * nf :].T,
        g_b[:nf].T,
        g_b[nf : 2 * nf].T,
        g_c.T,
        gains[:d],
        gains[d : d + h],
        gains[d + h : d + 2 * h],
        gains[d + 2 * h : 2 * d + 2 * h],
        gains[2 * d + 2 * h : 3 * d + 2 * h],
        gains[3 * d + 2 * h : 4 * d + 2 * h],
    )


def solution(mesh):
    split_rows = P("fsdp", None)
    split_cols = P(None, "fsdp")
    return jax.shard_map(
        functools.partial(shards, mesh.shape["fsdp"]),
        mesh=mesh,
        in_specs=(split_rows,) * 3 + (split_cols,) * 7 + (P(),) * 6,
        out_specs=(split_rows,) * 2 + (split_cols,) * 7 + (P(),) * 6,
        check_vma=False,
    )
```

```python
import functools
import math

import jax
import jax.numpy as jnp
from jax import lax
from jax.experimental import pallas as pl
from jax.experimental.pallas import tpu as pltpu
from jax.sharding import PartitionSpec as P

HEADS = 4
HEAD_DIM = 256
HALF = HEAD_DIM // 2
EPSILON = 1e-06
ROPE_BASE = 1000000.0
NEG_FILL = -1e30
QUERY_SCALE = 0.0625
GELU_C = math.sqrt(2.0 / math.pi)
GELU_A = 0.044715
BF = jnp.bfloat16
F32 = jnp.float32
QBLOCK = 256
ROW_BLOCK = 512
FF_BLOCK = 512
FFN_ROWS = 256
VMEM_LIMIT = 60 * 1024 * 1024
GRAD_VMEM = 32 * 1024 * 1024


def dot_nn(a, b):
    return lax.dot_general(a, b, (((1,), (0,)), ((), ())), preferred_element_type=F32)


def dot_nt(a, b):
    return lax.dot_general(a, b, (((1,), (1,)), ((), ())), preferred_element_type=F32)


def dot_tn(a, b):
    return lax.dot_general(a, b, (((0,), (0,)), ((), ())), preferred_element_type=F32)


def inv_rms(v):
    return lax.rsqrt(jnp.mean(v * v, axis=-1, keepdims=True) + EPSILON)


def row_sum(v):
    return jnp.sum(v, axis=0, keepdims=True)


def params(limit=VMEM_LIMIT):
    return pltpu.CompilerParams(dimension_semantics=("arbitrary",), vmem_limit_bytes=limit)


def const_spec(shape):
    zeros = (0,) * len(shape)
    return pl.BlockSpec(shape, lambda i, *_: zeros, pipeline_mode=pl.Buffered(1))


def cost(flops, nbytes, trans=0):
    return pl.CostEstimate(flops=int(flops) // 32, bytes_accessed=int(nbytes) // 32, transcendentals=int(trans) // 32)


def pack_qkv(place_ref, own_ref, other_ref, w_ref, nq, nk):
    half = own_ref.shape[0]
    width = HEADS * HEAD_DIM
    per = 16 // nk

    def group(g, carry):
        keys = []
        values = []
        for e in range(per):
            j = g * per + e
            at = place_ref[j]
            low = jnp.minimum(at, half - 1)
            high = jnp.maximum(at - half, 0)
            block = jnp.where(at < half, own_ref[low].astype(F32), other_ref[high].astype(F32))
            w_ref[pl.ds(pl.multiple_of(j * nq, nq), nq), :] = block[:nq].astype(BF)
            keys.append(block[nq : nq + nk])
            values.append(block[nq + nk :])
        at = pl.multiple_of(width + g * 16, 16)
        w_ref[pl.ds(at, 16), :] = jnp.concatenate(keys, axis=0).astype(BF)
        at = pl.multiple_of(width + HEAD_DIM + g * 16, 16)
        w_ref[pl.ds(at, 16), :] = jnp.concatenate(values, axis=0).astype(BF)
        return carry

    lax.fori_loop(0, 2 * half // per, group, 0)


def qkv_kernel(packed, place_ref, x_ref, *refs):
    if packed is None:
        w_ref, gi_ref, gq_ref, gk_ref, cos_ref, sin_ref, q_ref, k_ref, v_ref, s_ref, n_ref = refs
    else:
        own_ref, other_ref, gi_ref, gq_ref, gk_ref, cos_ref, sin_ref, q_ref, k_ref, v_ref, s_ref, n_ref, w_ref = refs

        @pl.when(pl.program_id(0) == 0)
        def _():
            pack_qkv(place_ref, own_ref, other_ref, w_ref, *packed)

    x = x_ref[...].astype(F32)
    normed = (x * inv_rms(x) * gi_ref[...]).astype(BF)
    n_ref[...] = normed
    cos = cos_ref[...]
    sin = sin_ref[...]
    width = HEADS * HEAD_DIM
    v_ref[...] = dot_nt(normed, w_ref[width + HEAD_DIM :, :]).astype(BF)
    lane = lax.broadcasted_iota(jnp.int32, s_ref.shape, 1)
    saved = jnp.zeros(s_ref.shape, F32)
    for h in range(HEADS + 1):
        raw = dot_nt(normed, w_ref[h * HEAD_DIM : (h + 1) * HEAD_DIM, :])
        inv = inv_rms(raw)
        saved = jnp.where(lane == h, inv, saved)
        gain = gq_ref[...] * QUERY_SCALE if h < HEADS else gk_ref[...]
        y = raw * inv * gain
        y1 = y[:, :HALF]
        y2 = y[:, HALF:]
        out = q_ref.at[h] if h < HEADS else k_ref
        out[:, :HALF] = (y1 * cos - y2 * sin).astype(BF)
        out[:, HALF:] = (y2 * cos + y1 * sin).astype(BF)
    s_ref[...] = saved


def qkv_call(place, x, weights, packed, gi, gq, gk, cos, sin):
    rows, d = x.shape
    b = ROW_BLOCK
    width = HEADS * HEAD_DIM
    row = lambda n: pl.BlockSpec((b, n), lambda i, *_: (i, 0))
    sds = jax.ShapeDtypeStruct
    whole = sds((width + 2 * HEAD_DIM, d), BF)
    outs = [sds((HEADS, rows, HEAD_DIM), BF), sds((rows, HEAD_DIM), BF), sds((rows, HEAD_DIM), BF),
            sds((rows, 128), F32), sds((rows, d), BF)]
    out_specs = [pl.BlockSpec((HEADS, b, HEAD_DIM), lambda i, *_: (0, i, 0)), row(HEAD_DIM), row(HEAD_DIM), row(128),
                 row(d)]
    if packed is not None:
        outs.append(whole)
        out_specs.append(pl.BlockSpec(whole.shape, lambda i, *_: (0, 0)))
    result = pl.pallas_call(
        functools.partial(qkv_kernel, packed),
        grid_spec=pltpu.PrefetchScalarGridSpec(
            num_scalar_prefetch=1,
            grid=(rows // b,),
            in_specs=[row(d)] + [const_spec(w.shape) for w in weights]
            + [const_spec((1, d)), const_spec((1, HEAD_DIM)), const_spec((1, HEAD_DIM)), row(HALF), row(HALF)],
            out_specs=out_specs,
        ),
        out_shape=outs,
        compiler_params=params(),
        cost_estimate=cost(2 * rows * d * (width + 2 * HEAD_DIM), 12 * rows * d),
        name="qkv_rows",
    )(place, x, *weights, gi, gq, gk, cos, sin)
    return result if packed is not None else list(result) + [weights[0]]


def attend_kernel(blocks, first_ref, q_ref, k_ref, v_ref, start_ref, p_ref, o_ref):
    i = pl.program_id(0)
    qb = lax.rem(i, blocks)
    first = first_ref[i]
    count = qb + 1 - first
    m_rows = HEADS * QBLOCK
    for n in range(1, blocks + 1):

        @pl.when(count == n)
        def _():
            base = pl.multiple_of(first * QBLOCK, QBLOCK)
            window = pl.ds(base, n * QBLOCK)
            q = q_ref[...].reshape(m_rows, HEAD_DIM)
            scores = dot_nt(q, k_ref[window, :])
            col = lax.broadcasted_iota(jnp.int32, scores.shape, 1) + base
            row = lax.broadcasted_iota(jnp.int32, (QBLOCK, 1), 0) + qb * QBLOCK
            row = jnp.concatenate([row] * HEADS, axis=0)
            start = jnp.concatenate([start_ref[...]] * HEADS, axis=0)
            scores = jnp.where((col >= start) & (col <= row), scores, NEG_FILL)
            e = jnp.exp(scores - jnp.max(scores, axis=-1, keepdims=True))
            probs = (e * (1.0 / jnp.sum(e, axis=-1, keepdims=True))).astype(BF)
            p_ref[0, :, : n * QBLOCK] = probs
            out = dot_nn(probs, v_ref[window, :]).astype(BF)
            for h in range(HEADS):
                o_ref[:, h * HEAD_DIM : (h + 1) * HEAD_DIM] = out[h * QBLOCK : (h + 1) * QBLOCK]


def attend_call(first, q, k, v, start, slots):
    rows = k.shape[0]
    slot_rows = rows // slots
    blocks = slot_rows // QBLOCK
    width = HEADS * HEAD_DIM
    slot = pl.BlockSpec((slot_rows, HEAD_DIM), lambda i, *_: (i // blocks, 0))
    return pl.pallas_call(
        functools.partial(attend_kernel, blocks),
        grid_spec=pltpu.PrefetchScalarGridSpec(
            num_scalar_prefetch=1,
            grid=(slots * blocks,),
            in_specs=[pl.BlockSpec((HEADS, QBLOCK, HEAD_DIM), lambda i, *_: (0, i, 0)), slot, slot,
                      pl.BlockSpec((QBLOCK, 1), lambda i, *_: (i, 0))],
            out_specs=[pl.BlockSpec((1, HEADS * QBLOCK, slot_rows), lambda i, *_: (i, 0, 0)),
                       pl.BlockSpec((QBLOCK, width), lambda i, *_: (i, 0))],
        ),
        out_shape=[jax.ShapeDtypeStruct((slots * blocks, HEADS * QBLOCK, slot_rows), BF),
                   jax.ShapeDtypeStruct((rows, width), BF)],
        compiler_params=params(),
        cost_estimate=cost(4 * rows * slot_rows * width * 5 // 8, 2 * rows * slot_rows * HEADS + 8 * rows * width,
                           rows * slot_rows * HEADS * 5 // 8),
        name="attend_rows",
    )(first, q, k, v, start)


def load_weights(place_ref, srcs, wo_s, wg_s, wu_s, wd_s, sem, nf, nq):
    b_own, b_other, c_own, c_other = srcs
    half = b_own.shape[0]
    copies = []
    for n, (b, c) in enumerate(((b_own, c_own), (b_other, c_other))):
        to = pl.ds(n * half, half)
        copies.append(pltpu.make_async_copy(b.at[:, pl.ds(0, nf), :], wg_s.at[to], sem.at[3 * n]))
        copies.append(pltpu.make_async_copy(b.at[:, pl.ds(nf, nf), :], wu_s.at[to], sem.at[3 * n + 1]))
        copies.append(pltpu.make_async_copy(c, wd_s.at[to], sem.at[3 * n + 2]))
    copies.append(pltpu.make_async_copy(b_own.at[:, pl.ds(2 * nf, nq), :], wo_s.at[pl.ds(0, half)], sem.at[6]))
    copies.append(pltpu.make_async_copy(b_other.at[:, pl.ds(2 * nf, nq), :], wo_s.at[pl.ds(half, half)], sem.at[7]))
    return copies


def ffn_kernel(slot_rows, packed, total_ref, place_ref, a_ref, x_ref, og_ref, *refs):
    if packed is None:
        wo_ref, wg_ref, wu_ref, wd_ref = refs[:4]
        refs = refs[4:]
    else:
        srcs = refs[:4]
        wo_ref, wo_s, wg_s, wu_s, wd_s, sem = refs[-6:]
        refs = refs[4:-6]
        flat = lambda r: r.reshape(r.shape[0] * r.shape[1], r.shape[2])
        wg_ref, wu_ref, wd_ref = flat(wg_s), flat(wu_s), flat(wd_s)
        copies = load_weights(place_ref, srcs, wo_s, wg_s, wu_s, wd_s, sem, *packed)

        @pl.when(pl.program_id(0) == 0)
        def _():
            for copy in copies[::-1]:
                copy.start()
            copies[7].wait()
            copies[6].wait()
            nq = packed[1]
            for j in range(wo_s.shape[0]):
                wo_ref[j * nq : (j + 1) * nq, :] = wo_s[place_ref[j]]
            for copy in copies[:6]:
                copy.wait()

    (ga_ref, gf_ref, go_ref, out_ref, wide_ref, fin_ref, gfo_ref, gb_ref, gatt_ref, gm_ref, dg_ref,
     gate_s, up_s) = refs
    i = pl.program_id(0)
    b = x_ref.shape[0]
    ff = wg_ref.shape[0]

    @pl.when(i == 0)
    def _():
        dg_ref[...] = jnp.zeros_like(dg_ref)

    branch = dot_nn(a_ref[...], wo_ref[...])
    s_b = inv_rms(branch)
    nb = branch * s_b
    middle = x_ref[...].astype(F32) + nb * ga_ref[...]
    s_m = inv_rms(middle)
    nm = middle * s_m
    ffn_in = (nm * gf_ref[...]).astype(BF)
    fin_ref[...] = ffn_in

    gate_s[...] = dot_nt(ffn_in, wg_ref[...])
    up_s[...] = dot_nt(ffn_in, wu_ref[...])
    gate = gate_s[...]
    t = jnp.tanh(gate * (GELU_C + (GELU_C * GELU_A) * (gate * gate)))
    hidden = (0.5 * gate * (1.0 + t) * up_s[...]).astype(BF)
    wide_ref[:, 2 * ff :] = hidden
    ffn_out = dot_nn(hidden, wd_ref[...])
    s_f = inv_rms(ffn_out)
    nf = ffn_out * s_f
    out_ref[...] = (middle + nf * go_ref[...]).astype(BF)

    per_slot = slot_rows // b
    row = lax.broadcasted_iota(jnp.int32, (b, 1), 0) + lax.rem(i, per_slot) * b
    live = row < total_ref[i // per_slot]
    upstream = jnp.where(live, og_ref[...].astype(F32), 0.0)
    dg_fo = row_sum(upstream * nf)
    scaled = upstream * go_ref[...]
    gfo = (s_f * (scaled - nf * jnp.mean(scaled * nf, axis=-1, keepdims=True))).astype(BF)
    gfo_ref[...] = gfo
    gh = dot_nt(gfo, wd_ref[...])
    gate = gate_s[...]
    sq = gate * gate
    t = jnp.tanh(gate * (GELU_C + (GELU_C * GELU_A) * sq))
    half_t = 0.5 + 0.5 * t
    slope = half_t + (0.5 * gate) * (1.0 - t * t) * (GELU_C + (3.0 * GELU_C * GELU_A) * sq)
    gg = (gh * up_s[...] * slope).astype(BF)
    gu = (gh * (gate * half_t)).astype(BF)
    wide_ref[:, :ff] = gg
    wide_ref[:, ff : 2 * ff] = gu
    gfin = dot_nn(gg, wg_ref[...]) + dot_nn(gu, wu_ref[...])
    dg_fi = row_sum(gfin * nm)
    scaled = gfin * gf_ref[...]
    gm = upstream + s_m * (scaled - nm * jnp.mean(scaled * nm, axis=-1, keepdims=True))
    gm_ref[...] = gm
    dg_at = row_sum(gm * nb)
    scaled = gm * ga_ref[...]
    gb = (s_b * (scaled - nb * jnp.mean(scaled * nb, axis=-1, keepdims=True))).astype(BF)
    gb_ref[...] = gb
    gatt_ref[...] = dot_nt(gb, wo_ref[...]).astype(BF)
    dg_ref[0:1, :] += dg_fo
    dg_ref[1:2, :] += dg_fi
    dg_ref[2:3, :] += dg_at


def ffn_call(total, place, attended, x, og, weights, packed, ff, ga, gf, go, slots):
    rows, d = x.shape
    width = attended.shape[1]
    b = FFN_ROWS
    row = lambda n: pl.BlockSpec((b, n), lambda i, *_: (i, 0))
    vec = const_spec((1, d))
    sds = jax.ShapeDtypeStruct
    scratch = [pltpu.VMEM((b, ff), F32), pltpu.VMEM((b, ff), F32)]
    if packed is None:
        weight_specs = [const_spec(w.shape) for w in weights]
    else:
        nf, nq = packed
        weight_specs = [pl.BlockSpec(memory_space=pl.ANY)] * 4
        scratch += [pltpu.VMEM((width, d), BF), pltpu.VMEM((width // nq, nq, d), BF)]
        scratch += [pltpu.VMEM((ff // nf, nf, d), BF)] * 3 + [pltpu.SemaphoreType.DMA((8,))]
    return pl.pallas_call(
        functools.partial(ffn_kernel, rows // slots, packed),
        grid_spec=pltpu.PrefetchScalarGridSpec(
            num_scalar_prefetch=2,
            grid=(rows // b,),
            in_specs=[row(width), row(d), row(d)] + weight_specs + [vec, vec, vec],
            out_specs=[row(d), row(3 * ff), row(d), row(d), row(d), row(width), row(d),
                       pl.BlockSpec((8, d), lambda i, *_: (0, 0))],
            scratch_shapes=scratch,
        ),
        out_shape=[sds((rows, d), BF), sds((rows, 3 * ff), BF), sds((rows, d), BF), sds((rows, d), BF),
                   sds((rows, d), BF), sds((rows, width), BF), sds((rows, d), F32), sds((8, d), F32)],
        compiler_params=params(),
        cost_estimate=cost(4 * rows * d * (width + 3 * ff), rows * (6 * ff + 12 * d), 2 * rows * ff),
        name="ffn_rows",
    )(total, place, attended, x, og, *weights, ga, gf, go)


def wide_grad_kernel(chunks, left_ref, r_ref, own_ref, other_ref):
    grads = dot_tn(left_ref[...], r_ref[...]).astype(BF).reshape(own_ref.shape)
    own = lax.rem(pl.program_id(0), chunks) < chunks // 2

    @pl.when(own)
    def _():
        own_ref[...] = grads

    @pl.when(jnp.logical_not(own))
    def _():
        other_ref[...] = grads


def wide_grad_call(wide, begin, many, right, ff, nf, total):
    rows, d = right.shape
    chunks = ff // FF_BLOCK
    half = ff // nf // 2
    last = chunks // 2 - 1
    out = jax.ShapeDtypeStruct((half, total, d), BF)
    block = (FF_BLOCK // nf, nf, d)
    return pl.pallas_call(
        functools.partial(wide_grad_kernel, chunks),
        grid=(chunks * many,),
        in_specs=[pl.BlockSpec((rows, FF_BLOCK), lambda i: (0, begin * chunks + i)), const_spec(right.shape)],
        out_specs=[pl.BlockSpec(block, lambda i: (jnp.minimum(lax.rem(i, chunks), last), i // chunks, 0)),
                   pl.BlockSpec(block, lambda i: (jnp.maximum(lax.rem(i, chunks) - last - 1, 0), i // chunks, 0))],
        out_shape=[out, out],
        compiler_params=params(GRAD_VMEM),
        cost_estimate=cost(2 * rows * ff * many * d, 2 * rows * ff * many),
        name="wide_grads",
    )(wide, right)


def out_grad_kernel(owner_ref, a_ref, r_ref, before_own, before_other, own_ref, other_ref, sum_s):
    half, nq, d = own_ref.shape
    sum_s[...] = dot_tn(a_ref[...], r_ref[...])
    for j in range(2 * half):
        rows = sum_s[pl.ds(pl.multiple_of(owner_ref[j] * nq, nq), nq), :].astype(BF)
        if j < half:
            own_ref[j] = rows
        else:
            other_ref[j - half] = rows


def out_grad_call(owner, attended, gb, before, nq):
    rows, width = attended.shape
    half, total, d = before[0].shape
    place = pl.BlockSpec((half, nq, d), lambda i, *_: (0, total // nq - 1, 0))
    return pl.pallas_call(
        out_grad_kernel,
        grid_spec=pltpu.PrefetchScalarGridSpec(
            num_scalar_prefetch=1,
            grid=(1,),
            in_specs=[const_spec(attended.shape), const_spec(gb.shape), pl.BlockSpec(memory_space=pl.ANY),
                      pl.BlockSpec(memory_space=pl.ANY)],
            out_specs=[place, place],
            scratch_shapes=[pltpu.VMEM((width, d), F32)],
        ),
        out_shape=[jax.ShapeDtypeStruct(before[0].shape, BF)] * 2,
        input_output_aliases={3: 0, 4: 1},
        compiler_params=params(GRAD_VMEM),
        cost_estimate=cost(2 * rows * width * d, 2 * rows * width),
        name="out_grads",
    )(owner, attended, gb, *before)


def qkv_grad_kernel(owner_ref, gq_ref, gk_ref, gv_ref, n_ref, w_ref, gi_ref, own_ref, other_ref, dg_ref, sum_s):
    i = pl.program_id(0)
    half, total, d = own_ref.shape
    nk = HEAD_DIM // (2 * half)
    nq = total - 2 * nk
    step = gq_ref.shape[1]
    width = HEADS * HEAD_DIM
    last = width // step

    @pl.when(i < last)
    def _():
        sum_s[pl.ds(pl.multiple_of(i * step, step), step), :] = dot_tn(gq_ref[...], n_ref[...])

    @pl.when(i == last)
    def _():
        sum_s[width:, :] = dot_tn(jnp.concatenate([gk_ref[...], gv_ref[...]], axis=1), n_ref[...])
        dg = row_sum(sum_s[...] * w_ref[...].astype(F32)) / gi_ref[...]
        dg_ref[...] = jnp.broadcast_to(dg, dg_ref.shape)
        for j in range(2 * half):
            at = owner_ref[j]
            block = jnp.concatenate(
                [
                    sum_s[pl.ds(pl.multiple_of(at * nq, nq), nq), :],
                    sum_s[pl.ds(pl.multiple_of(width + at * nk, nk), nk), :],
                    sum_s[pl.ds(pl.multiple_of(width + HEAD_DIM + at * nk, nk), nk), :],
                ],
                axis=0,
            ).astype(BF)
            if j < half:
                own_ref[j] = block
            else:
                other_ref[j - half] = block


def qkv_grad_call(owner, gq, gk, gv, normed, w_qkv, gi, total):
    rows, d = normed.shape
    half = owner.shape[0] // 2
    step = 2 * HEAD_DIM
    last = HEADS * HEAD_DIM // step
    out = pl.BlockSpec((half, total, d), lambda i, *_: (0, 0, 0))
    return pl.pallas_call(
        qkv_grad_kernel,
        grid_spec=pltpu.PrefetchScalarGridSpec(
            num_scalar_prefetch=1,
            grid=(last + 1,),
            in_specs=[pl.BlockSpec((rows, step), lambda i, *_: (0, jnp.minimum(i, last - 1))),
                      const_spec(gk.shape), const_spec(gv.shape), const_spec(normed.shape), const_spec(w_qkv.shape),
                      const_spec(gi.shape)],
            out_specs=[out, out, pl.BlockSpec((8, d), lambda i, *_: (0, 0))],
            scratch_shapes=[pltpu.VMEM(((HEADS + 2) * HEAD_DIM, d), F32)],
        ),
        out_shape=[jax.ShapeDtypeStruct((half, total, d), BF)] * 2 + [jax.ShapeDtypeStruct((8, d), F32)],
        compiler_params=params(GRAD_VMEM),
        cost_estimate=cost(2 * rows * d * (HEADS + 2) * HEAD_DIM, 4 * rows * HEADS * HEAD_DIM),
        name="qkv_grads",
    )(owner, gq, gk, gv, normed, w_qkv, gi)


def rope_back_halves(g1, g2, cos, sin):
    return g1 * cos + g2 * sin, g2 * cos - g1 * sin


def norm_rope_back(grad, rotated, inv, gain, cos, sin, scale):
    m = jnp.mean(grad * rotated, axis=-1, keepdims=True)
    dy1, dy2 = rope_back_halves(grad[:, :HALF], grad[:, HALF:], cos, sin)
    u1, u2 = rope_back_halves(rotated[:, :HALF], rotated[:, HALF:], cos, sin)
    dy = jnp.concatenate([dy1, dy2], axis=1) * scale
    n = jnp.concatenate([u1, u2], axis=1) * ((1.0 / scale) / gain)
    return inv * (dy * gain - n * m), row_sum(dy * n)


def attend_back_kernel(blocks, offset, kept, first_ref, p_ref, q_ref, k_ref, v_ref, do_ref, s_ref, cos_ref, sin_ref,
                       gq_ref, gk_ref, *rest):
    gqr_ref, gkr_ref, gv_ref, dg_ref, dq_s, dk_s, dv_s = rest[kept:]
    i = pl.program_id(0)
    qb = i
    first = first_ref[offset + i]
    count = qb + 1 - first
    m_rows = HEADS * QBLOCK

    @pl.when(i == 0)
    def _():
        dg_ref[...] = jnp.zeros_like(dg_ref)

    @pl.when(qb == 0)
    def _():
        dk_s[...] = jnp.zeros_like(dk_s)
        dv_s[...] = jnp.zeros_like(dv_s)

    for n in range(1, blocks + 1):

        @pl.when(count == n)
        def _():
            base = pl.multiple_of(first * QBLOCK, QBLOCK)
            window = pl.ds(base, n * QBLOCK)
            do = jnp.concatenate([do_ref[:, h * HEAD_DIM : (h + 1) * HEAD_DIM] for h in range(HEADS)], axis=0)
            q = q_ref[...].reshape(m_rows, HEAD_DIM)
            probs = p_ref[0, :, : n * QBLOCK]
            dp = dot_nt(do, v_ref[window, :])
            pf = probs.astype(F32)
            total = jnp.sum(pf * dp, axis=-1, keepdims=True)
            ds = (pf * (dp - total)).astype(BF)
            dq_s[...] = dot_nn(ds, k_ref[window, :])
            dk_s[window, :] += dot_tn(ds, q)
            dv_s[window, :] += dot_tn(probs, do)

    rows = pl.ds(pl.multiple_of(qb * QBLOCK, QBLOCK), QBLOCK)
    cos = cos_ref[rows, :]
    sin = sin_ref[rows, :]
    inv = s_ref[rows, :]
    for h in range(HEADS):
        grad, dg = norm_rope_back(dq_s[h * QBLOCK : (h + 1) * QBLOCK, :], q_ref[h].astype(F32), inv[:, h : h + 1],
                                  gq_ref[...], cos, sin, QUERY_SCALE)
        gqr_ref[:, h * HEAD_DIM : (h + 1) * HEAD_DIM] = grad.astype(BF)
        dg_ref[0:1, :] += dg

    @pl.when(qb == blocks - 1)
    def _():
        gv_ref[...] = dv_s[...].astype(BF)
        grad, dg = norm_rope_back(dk_s[...], k_ref[...].astype(F32), s_ref[:, HEADS : HEADS + 1], gk_ref[...],
                                  cos_ref[...], sin_ref[...], 1.0)
        gkr_ref[...] = grad.astype(BF)
        dg_ref[1:2, :] += dg


def attend_back_call(first, p, q, k, v, do, s, cos, sin, gq, gk, slots, which, previous):
    rows = k.shape[0]
    slot_rows = rows // slots
    blocks = slot_rows // QBLOCK
    width = HEADS * HEAD_DIM
    base = which * blocks
    slot = lambda n: pl.BlockSpec((slot_rows, n), lambda i, *_: (which, 0))
    block = lambda n: pl.BlockSpec((QBLOCK, n), lambda i, *_: (base + i, 0))
    sds = jax.ShapeDtypeStruct
    kept = () if previous is None else tuple(previous)
    return pl.pallas_call(
        functools.partial(attend_back_kernel, blocks, base, len(kept)),
        grid_spec=pltpu.PrefetchScalarGridSpec(
            num_scalar_prefetch=1,
            grid=(blocks,),
            in_specs=[pl.BlockSpec((1, HEADS * QBLOCK, slot_rows), lambda i, *_: (base + i, 0, 0)),
                      pl.BlockSpec((HEADS, QBLOCK, HEAD_DIM), lambda i, *_: (0, base + i, 0)),
                      slot(HEAD_DIM), slot(HEAD_DIM), block(width), slot(128), slot(HALF), slot(HALF),
                      const_spec((1, HEAD_DIM)), const_spec((1, HEAD_DIM))]
            + [pl.BlockSpec(memory_space=pl.ANY)] * len(kept),
            out_specs=[block(width), slot(HEAD_DIM), slot(HEAD_DIM), pl.BlockSpec((8, HEAD_DIM), lambda i, *_: (0, 0))],
            scratch_shapes=[pltpu.VMEM((HEADS * QBLOCK, HEAD_DIM), F32), pltpu.VMEM((slot_rows, HEAD_DIM), F32),
                            pltpu.VMEM((slot_rows, HEAD_DIM), F32)],
        ),
        out_shape=[sds((rows, width), BF), sds((rows, HEAD_DIM), BF), sds((rows, HEAD_DIM), BF),
                   sds((8, HEAD_DIM), F32)],
        input_output_aliases={11 + j: j for j in range(len(kept))},
        compiler_params=params(),
        cost_estimate=cost(8 * slot_rows * slot_rows * width * 5 // 8,
                           2 * slot_rows * slot_rows * HEADS + 12 * slot_rows * width),
        name="attend_back_rows",
    )(first, p, q, k, v, do, s, cos, sin, gq, gk, *kept)


def input_back_kernel(gq_ref, gk_ref, gv_ref, x_ref, gm_ref, w_ref, gi_ref, gx_ref):
    width = HEADS * HEAD_DIM
    gn = dot_nn(gq_ref[...], w_ref[:width, :])
    gn += dot_nn(gk_ref[...], w_ref[width : width + HEAD_DIM, :])
    gn += dot_nn(gv_ref[...], w_ref[width + HEAD_DIM :, :])
    x = x_ref[...].astype(F32)
    inv = inv_rms(x)
    n = x * inv
    scaled = gn * gi_ref[...]
    gx = inv * (scaled - n * jnp.mean(scaled * n, axis=-1, keepdims=True))
    gx_ref[...] = (gm_ref[...] + gx).astype(BF)


def input_back_call(gq, gk, gv, x, gm, w_qkv, gi):
    rows, d = x.shape
    b = ROW_BLOCK
    row = lambda n: pl.BlockSpec((b, n), lambda i: (i, 0))
    return pl.pallas_call(
        input_back_kernel,
        grid=(rows // b,),
        in_specs=[row(gq.shape[1]), row(HEAD_DIM), row(HEAD_DIM), row(d), row(d), const_spec(w_qkv.shape),
                  const_spec((1, d))],
        out_specs=row(d),
        out_shape=jax.ShapeDtypeStruct((rows, d), BF),
        compiler_params=params(),
        cost_estimate=cost(2 * rows * d * w_qkv.shape[0], 14 * rows * d),
        name="input_back_rows",
    )(gq, gk, gv, x, gm, w_qkv, gi)


def level_list(count):
    levels = [(1, 2)]
    stride = 2
    while stride < count:
        size = 4 if count // stride >= 4 else 2
        levels.append((stride, size))
        stride *= size
    return levels


def send(x, count, offset):
    return lax.ppermute(x, "fsdp", [(i, i ^ offset) for i in range(count)])


def swap(x, count, level):
    stride, size = level
    return [send(x, count, k * stride) for k in range(1, size)]


def block_offsets(count):
    offsets = [0]
    for stride, size in level_list(count)[::-1]:
        offsets = [o ^ (k * stride) for k in range(size) for o in offsets]
    return offsets


def tie(values, *after):
    return lax.optimization_barrier((values, after))[0]


def open_blocks(x, levels):
    return x.reshape((1,) * len(levels) + x.shape)


def join(own, received, axis):
    return jnp.concatenate([own] + list(received), axis=axis)


def part(g, axis, k):
    return lax.slice_in_dim(g, k, k + 1, axis=axis)


def give(g, count, level, axis):
    stride, size = level
    return [send(part(g, axis, k).astype(BF), count, k * stride) for k in range(1, size)]


def add_up(g, received, axis, kind=BF):
    total = part(g, axis, 0).astype(F32)
    for r in received:
        total = total + r.astype(F32)
    return total.astype(kind)


def slot_layout(lengths, row_count):
    seq_ends = jnp.cumsum(lengths, axis=1, dtype=jnp.int32)
    rows = lax.broadcasted_iota(jnp.int32, (lengths.shape[0], row_count), 1)
    passed = rows[:, :, None] >= seq_ends[:, None, :]
    start = jnp.sum(jnp.where(passed, lengths[:, None, :], 0), axis=2, dtype=jnp.int32)
    return start, rows - start, seq_ends[:, -1]


def shards(count, tokens, out_grad, seq_lengths, w_query, w_key, w_value, w_output, w_gate, w_up, w_down,
           gain_input, gain_query, gain_key, gain_attn, gain_ffn_in, gain_ffn_out):
    slots = seq_lengths.shape[0]
    rows, d = tokens.shape
    slot_rows = rows // slots
    me = lax.axis_index("fsdp")
    levels = level_list(count)
    depth = len(levels)
    core, near, far = levels[0], levels[1], levels[2:]
    order = block_offsets(count)
    inverse = [0] * count
    for j, o in enumerate(order):
        inverse[o] = j
    place = jnp.array(inverse, jnp.int32)[jnp.arange(count, dtype=jnp.int32) ^ me]
    owner = jnp.array(order, jnp.int32) ^ me
    nq, nk, nf = w_query.shape[1], w_key.shape[1], w_gate.shape[1]

    aligned = nq % 16 == 0 and nk == 8 and nf % 16 == 0
    na = nq + 2 * nk

    a = open_blocks(jnp.concatenate([w_query.T, w_key.T, w_value.T], axis=0), levels)
    b = open_blocks(jnp.concatenate([w_gate.T, w_up.T, w_output.T], axis=0), levels)
    c = open_blocks(w_down.T, levels)
    start, position, total = slot_layout(seq_lengths, slot_rows)

    for n in range(depth - 1, 1, -1):
        a = join(a, swap(a, count, levels[n]), n)
    c = join(c, swap(c, count, near), 1)
    for n in range(depth - 1, 1, -1):
        b = join(b, swap(b, count, levels[n]), n)
    inv_freq = jnp.exp(lax.iota(jnp.int32, HALF).astype(F32) * (-2.0 * math.log(ROPE_BASE) / HEAD_DIM))
    phases = position.reshape(rows, 1).astype(F32) * inv_freq[None, :]
    received = swap(a, count, near)
    cos = jnp.cos(phases)
    sin = jnp.sin(phases)
    received, cos, sin = lax.optimization_barrier((received, cos, sin))
    a = join(a, received, 1)
    b = tie(b, a, c)
    b_near = swap(b, count, near)
    a_core = swap(a, count, core)[0]
    half = count // 2
    a, a_core = a.reshape((half, na, d)), a_core.reshape((half, na, d))
    first = (start[:, ::QBLOCK] // QBLOCK).reshape(-1)
    start_col = start.reshape(rows, 1)
    gi, gq, gk = gain_input[None], gain_query[None], gain_key[None]
    if aligned:
        a_weights, a_packed = (a, a_core), (nq, nk)
    else:
        a = jnp.concatenate([a, a_core], axis=0)[place]
        w_qkv = jnp.concatenate(
            [a[:, :nq].reshape(-1, d), a[:, nq : nq + nk].reshape(-1, d), a[:, nq + nk :].reshape(-1, d)], axis=0
        )
        a_weights, a_packed = (w_qkv,), None

    a_weights, b = lax.optimization_barrier((a_weights, b))
    for n in range(2, depth - 1):
        c = join(c, swap(c, count, levels[n]), n)
    c_far, c_late = [], []
    if depth > 2:
        stride, size = levels[-1]
        early = tie(c, b)
        c_far = [send(early, count, step * stride) for step in range(1, min(size, 3))]
    q, k, v, s, normed, w_qkv = qkv_call(place, tokens, a_weights, a_packed, gi, gq, gk, cos, sin)
    if depth > 2:
        q, late = lax.optimization_barrier((q, c))
        c_late = [send(late, count, step * stride) for step in range(3, size)]
    p, attended = attend_call(first, q, k, v, start_col, slots)

    b_near, c_far = tie((b_near, c_far + c_late), attended)
    b = join(b, b_near, 1)
    b_core = swap(b, count, core)[0]
    c = join(c, c_far, depth - 1)
    c_core = swap(c, count, core)[0]
    b, b_core = b.reshape((half, 2 * nf + nq, d)), b_core.reshape((half, 2 * nf + nq, d))
    c, c_core = c.reshape((half, nf, d)), c_core.reshape((half, nf, d))
    if aligned:
        b_weights, b_packed = (b, b_core, c, c_core), (nf, nq)
    else:
        b = jnp.concatenate([b, b_core], axis=0)
        b_weights = (b[:, 2 * nf :][place].reshape(-1, d), b[:, :nf].reshape(-1, d), b[:, nf : 2 * nf].reshape(-1, d),
                     jnp.concatenate([c, c_core], axis=0).reshape(-1, d))
        b_packed = None
    out, wide, fin, gfo, gb, gatt, gm, dg_ffn = ffn_call(
        total, place, attended, tokens, out_grad, b_weights, b_packed, count * nf, gain_attn[None],
        gain_ffn_in[None], gain_ffn_out[None], slots
    )

    sizes = tuple(size for _, size in levels[1:])
    spread = lambda g: g.reshape(sizes + g.shape[1:])
    halves = lambda g: (g[:half], g[half:])
    if aligned:
        gb_pair = wide_grad_call(wide, 0, 2, fin, count * nf, nf, 2 * nf + nq)
        gb_pair = out_grad_call(owner, attended, gb, gb_pair, nq)
    else:
        g_out = dot_tn(attended, gb).astype(BF).reshape(count, nq, d)[owner]
        g_wide = wide_grad_call(wide, 0, 2, fin, count * nf, nf, 2 * nf)
        gb_pair = [jnp.concatenate(both, axis=1) for both in zip(g_wide, halves(g_out))]
    gb_all, gb_other = gb_pair
    stride, size = near
    gb_core = send(gb_other, count, core[0])
    gc_all, gc_other = wide_grad_call(wide, 2, 1, tie(gfo, gb_other), count * nf, nf, nf)
    gb_core = tie(gb_core, gc_all)
    gb_all = spread((gb_all.astype(F32) + gb_core.astype(F32)).astype(BF))
    ask = lambda k: send(part(gb_all, 0, k), count, k * stride)
    gb_near = [ask(k) for k in range(1, min(size, 3))]
    gc_core = send(gc_other, count, core[0])

    p = tie(p, gb_all)
    back = None
    dg_att = 0.0
    for which in range(slots):
        back = attend_back_call(first, p, q, k, v, gatt, s, cos, sin, gq, gk, slots, which, back)
        dg_att = dg_att + back[3]
        back = back[:3]
        if which == 0:
            gb_near, gc_core = tie((gb_near, gc_core), back[0])
            gc_all = spread((gc_all.astype(F32) + gc_core.astype(F32)).astype(BF))
            back = tie(back, gb_near, gc_all)
            gc_far, gc_late = [], []
            if depth > 2:
                give_c = lambda g, step: send(part(g, depth - 2, step), count, step * levels[-1][0])
                gc_far = [give_c(gc_all, step) for step in range(1, min(levels[-1][1], 3))]
            gb_all = tie(gb_all, gb_near, gc_all)
            gb_last = [ask(k) for k in range(3, size)]
    back, gb_last, gc_far, gc_rest = lax.optimization_barrier((back, gb_last, gc_far, gc_all))
    gqr, gkr, gv = back
    if depth > 2:
        gc_late = [give_c(gc_rest, step) for step in range(3, levels[-1][1])]
    if aligned:
        ga_all, ga_other, dg_in = qkv_grad_call(owner, gqr, gkr, gv, normed, w_qkv, gi, na)
    else:
        wg = lambda left, n: dot_tn(left, normed).astype(BF)
        whole = [wg(gqr, nq), wg(gkr, nk), wg(gv, nk)]
        dg_in = jnp.sum(jnp.concatenate(whole, axis=0).astype(F32) * w_qkv.astype(F32), axis=0, keepdims=True) / gi
        whole = [g.reshape(count, -1, d) for g in whole]
        ga_all, ga_other = halves(jnp.concatenate(whole, axis=1)[owner])
    gains = jnp.concatenate([dg_in[0], dg_att[0], dg_att[1], dg_ffn[2], dg_ffn[1], dg_ffn[0]])
    gains = jnp.pad(gains, (0, -gains.shape[0] % d)).reshape(-1, d)
    n_gain = gains.shape[0]

    def with_gains(g):
        high = gains.astype(BF)
        low = (gains - high.astype(F32)).astype(BF)
        return jnp.concatenate([g.astype(BF).reshape(-1, d), high, low], axis=0)

    def split_gains(message, shape):
        rest = message[-2 * n_gain :].astype(F32)
        return message[: -2 * n_gain].reshape(shape).astype(F32), rest[:n_gain] + rest[n_gain:]

    ga_core = send(with_gains(ga_other), count, core[0])
    gb_last = tie(gb_last, ga_other)
    gb_all = add_up(gb_all, gb_near + gb_last, 0)
    ga_core, gb_all = lax.optimization_barrier((ga_core, gb_all))
    received, more = split_gains(ga_core, ga_all.shape)
    ga_all = spread(ga_all.astype(F32) + received)
    gains = gains + more
    gb_late = []
    for n in range(1, depth):
        stride, size = levels[n]
        pieces = [part(ga_all, n - 1, step) for step in range(size)]
        messages = [send(with_gains(piece), count, step * stride) for step, piece in enumerate(pieces) if step]
        if n == 1:
            if depth > 2:
                far_stride, far_size = levels[2]
                give_far = lambda step: send(part(gb_all, 1, step), count, step * far_stride)
                gb_late = [give_far(step) for step in range(1, min(far_size, 3))]
            gm = tie(gm, ga_all, gb_all)
            grad_tokens = input_back_call(gqr, gkr, gv, tokens, gm, w_qkv, gi)
            messages, gb_late, gb_rest, gc_all, gc_late = tie((messages, gb_late, gb_all, gc_all, gc_late), grad_tokens)
            if depth > 2:
                gc_all = add_up(gc_all, gc_far + gc_late, depth - 2)
            if depth > 2:
                gb_late = gb_late + [send(part(gb_rest, 1, step), count, step * far_stride)
                                     for step in range(3, far_size)]
        ga_all = pieces[0]
        for message in messages:
            received, more = split_gains(message, ga_all.shape)
            ga_all = ga_all + received
            gains = gains + more
    for n in range(2, depth):
        received = gb_late if n == 2 else give(gb_all, count, levels[n], n - 1)
        gb_all = add_up(gb_all, received, n - 1, F32 if n == depth - 1 else BF)
    for n in range(depth - 2, 0, -1):
        gc_all = add_up(gc_all, give(gc_all, count, levels[n], n - 1), n - 1, F32 if n == 1 else BF)
    g_qkv = ga_all.reshape(nq + 2 * nk, d).astype(F32)
    g_b = gb_all.reshape(2 * nf + nq, d).astype(F32)
    g_c = gc_all.reshape(nf, d).astype(F32)
    gains = gains.reshape(-1)
    h = HEAD_DIM
    return (
        out,
        grad_tokens,
        g_qkv[:nq].T,
        g_qkv[nq : nq + nk].T,
        g_qkv[nq + nk :].T,
        g_b[2 * nf :].T,
        g_b[:nf].T,
        g_b[nf : 2 * nf].T,
        g_c.T,
        gains[:d],
        gains[d : d + h],
        gains[d + h : d + 2 * h],
        gains[d + 2 * h : 2 * d + 2 * h],
        gains[2 * d + 2 * h : 3 * d + 2 * h],
        gains[3 * d + 2 * h : 4 * d + 2 * h],
    )


def solution(mesh):
    split_rows = P("fsdp", None)
    split_cols = P(None, "fsdp")
    return jax.shard_map(
        functools.partial(shards, mesh.shape["fsdp"]),
        mesh=mesh,
        in_specs=(split_rows,) * 3 + (split_cols,) * 7 + (P(),) * 6,
        out_specs=(split_rows,) * 2 + (split_cols,) * 7 + (P(),) * 6,
        check_vma=False,
    )
```
